256 devices in a mesh: req: 32 (over x, z_hi, core), tp: 8 (over y, z_lo).
Axes of the slice: x: 4, y: 4, z: 8 (z_hi: 4, z_lo: 2; z = z_hi * 2 + z_lo), core: 2. Of those that a mesh axis runs over, the one named last changes fastest.
Arguments:
- queries: bfloat16 [8192, 5120], P('req', 'tp')
- suffix_keys: bfloat16 [8192, 5120], P('req', 'tp')
- suffix_values: bfloat16 [8192, 5120], P('req', 'tp'), may hold values from -6 to 6
- page_cache: bfloat16 [64, 128, 2, 5120], P('req', None, None, 'tp'), may hold values from -6 to 6
- page_table: int32 [2, 32], replicated, may hold values from 0 to 63, as said below
- suffix_lengths: int32 [32, 4], P('req'), may hold values from 1 to 128, 256 in all within a row
- request_group: int32 [32, 4], P('req'), may hold values from 0 to 1
- residual: bfloat16 [8192, 5120], P('req', 'tp'), may hold values from -6 to 6
- out_weight: bfloat16 [5120, 5120], P('tp'), may hold values from -0.3125 to 0.3125
- attn_gate: float32 [5120], P('tp'), may hold values from 0.5 to 2
- mod_shift: float32 [5120], P('tp'), may hold values from -3 to 3
- mod_scale: float32 [5120], P('tp'), may hold values from -0.5 to 1
Outputs:
- stream: bfloat16 [8192, 5120], P('req', 'tp')
- mlp_input: bfloat16 [8192, 5120], P('req', 'tp')
The draws below stay inside these ranges and needn't reach their ends.
Inputs may be any that keep to these rules, and one draw needn't show every extreme that they name: `page_table`: every slot 0 to 63 appears exactly once; slot s lies on req index s // 2. `suffix_lengths`: the lengths of one req index's requests sum to 256.
All inputs are finite; a program needn't handle non-finite values.
Results may differ from the reference program's by a relative error of at most 0.015.
Values may be sent and summed in bfloat16 or wider, within the bound.
No kernel may reach another device: no remote copies, remote signals or barrier semaphores. Data moves between devices by JAX's collectives and lax.ppermute only.
A program may use at most 128 MiB of HBM per device.

```python
import math
import jax
import jax.numpy as jnp
import numpy as np
from jax import lax

D = 5120
HEADS = 40
HS = 128
PAGE = 128
PAGES = 32
SPAN = 64
SLOTS_DEV = 2
REQ_DEV = 4
TOK_DEV = 256
GROUPS = 2
MOSTLEN = 128
TOKENS = 8192
N_REQ = 32


def common_keys(key):
    return jnp.clip(jax.random.normal(jax.random.fold_in(key, 11), (TOKENS, HEADS * HS), jnp.float32), -6.0, 6.0)


def draw_suffix_keys(key, part):
    return common_keys(key).astype(jnp.bfloat16)


def draw_queries(key, part):
    values = 2.5 * jnp.clip(jax.random.normal(jax.random.fold_in(key, 12), (TOKENS, HEADS * HS), jnp.float32), -6.0, 6.0)
    return values.astype(jnp.bfloat16)


def draw_page_table(key, part):
    order = jax.random.permutation(jax.random.fold_in(key, 13), GROUPS * PAGES)
    return order.astype(jnp.int32).reshape(GROUPS, PAGES)


def place_ends(result, key, low, top_value):
    longest = result.shape.index(max(result.shape))
    spots = []
    for shift in (0, 1):
        where = [jax.random.randint(jax.random.fold_in(key, axis), (), 0, length) for axis, length in enumerate(result.shape)]
        where[longest] = (where[longest] + shift) % result.shape[longest]
        spots.append(tuple(where))
    return result.at[spots[0]].set(low).at[spots[1]].set(top_value)


def steps_of(own_key, shape, pieces, smallest, high):
    loudness = 1.0
    for dim, parts in pieces:
        heights = jax.random.uniform(jax.random.fold_in(jax.random.fold_in(own_key, 6), dim), (parts,), jnp.float32, smallest / len(pieces), high / len(pieces))
        loudness = loudness * jnp.repeat(jnp.exp(heights), shape[dim] // parts).reshape((-1,) + (1,) * (len(shape) - 1 - dim))
    return loudness


def length_profile(count, total, most, skew):
    portions = [(1 << 20) // math.isqrt(grade ** skew) + 1 for grade in range(2, count + 1)]
    surplus, holding = total - most - (count - 1), [1] * (count - 1)
    while surplus > 0:
        free = [i for i in range(count - 1) if holding[i] < most]
        mass, remaining = sum([portions[i] for i in free]), surplus
        for i in free:
            more = min(most - holding[i], max(1, remaining * portions[i] // mass), surplus)
            holding[i] = holding[i] + more
            surplus = surplus - more
    return np.array([most] + holding)


def ragged_sizes(own_key, amount, total, reach, lean):
    if amount == 2:
        one = jax.random.randint(own_key, (), max(1, total - reach), min(reach, total - 1) + 1)
        return jnp.stack([one, total - one])
    tallies = jnp.asarray(length_profile(amount, total, reach, lean), jnp.int32)
    pairs = (amount - 1) // 2
    giver, taker = tallies[1:1 + 2 * pairs:2], tallies[2:2 + 2 * pairs:2]
    room = jnp.minimum(giver - 1, reach - taker)
    moved = jax.random.randint(jax.random.fold_in(own_key, 1), (pairs,), 0, 1 << 20) % (room + 1)
    tallies = tallies.at[1:1 + 2 * pairs:2].set(giver - moved).at[2:2 + 2 * pairs:2].set(taker + moved)
    return tallies[jax.random.permutation(jax.random.fold_in(own_key, 2), amount)]


def centred(rng, dims, scale, bound, shards=(), held_as=jnp.bfloat16):
    loudness = steps_of(rng, dims, shards, -0.22, 0.18) if shards else 1.0
    entries = jax.random.normal(rng, dims, jnp.float32) * scale * loudness
    return jnp.minimum(jnp.maximum(entries, -bound), bound).astype(held_as)


def setup_inputs(seed: int = 0) -> dict:
    keys = jax.random.split(jax.random.key(seed), 13)
    queries = draw_queries(jax.random.fold_in(keys[12], 71), 0)
    suffix_keys = draw_suffix_keys(jax.random.fold_in(keys[12], 71), 0)
    suffix_values = centred(keys[2], (TOKENS, HEADS * HS), 1.0, 6.0, ((0, 32), (1, 8)))
    page_cache = centred(keys[3], (N_REQ * SLOTS_DEV, PAGE, 2, HEADS * HS), 1.0, 6.0, ((0, 32), (3, 8)))
    page_table = draw_page_table(jax.random.fold_in(keys[12], 71), 0)
    suffix_lengths = jax.vmap(lambda own: ragged_sizes(own, REQ_DEV, TOK_DEV, MOSTLEN, 2))(jax.random.split(keys[5], N_REQ)).reshape((N_REQ, REQ_DEV)).astype(jnp.int32)
    request_group = place_ends(jax.random.randint(keys[6], (N_REQ, REQ_DEV), 0, GROUPS), jax.random.fold_in(keys[6], 1), 0, GROUPS - 1).astype(jnp.int32)
    residual = centred(keys[7], (TOKENS, D), 1.0, 6.0, ((0, 32), (1, 8)))
    out_weight = centred(keys[8], (HEADS * HS, D), (HEADS * HS // 16) ** -0.5, 0.3125, ((0, 8),))
    attn_gate = jnp.clip(0.5 + 1.5 * jax.random.uniform(keys[9], (D,), jnp.float32) ** steps_of(keys[9], (D,), ((0, 8),), -0.2, 0.2), 0.5, 2.0)
    mod_shift = centred(keys[10], (D,), 0.5, 3.0, ((0, 8),), jnp.float32)
    mod_scale = jnp.clip(-0.5 + 1.5 * jax.random.uniform(keys[11], (D,), jnp.float32) ** steps_of(keys[11], (D,), ((0, 8),), -0.2, 0.2), -0.5, 1.0)
    return dict(queries=queries, suffix_keys=suffix_keys, suffix_values=suffix_values, page_cache=page_cache, page_table=page_table, suffix_lengths=suffix_lengths, request_group=request_group, residual=residual, out_weight=out_weight, attn_gate=attn_gate, mod_shift=mod_shift, mod_scale=mod_scale)


def head_attention(query_head, key_head, value_head, prefix_key, prefix_value, same_request, prefix_visible):
    inv_sqrt = 1.0 / math.sqrt(HS)
    scores_suffix = jnp.dot(query_head, key_head.T, preferred_element_type=jnp.float32) * inv_sqrt
    scores_prefix = jnp.dot(query_head, prefix_key.T, preferred_element_type=jnp.float32) * inv_sqrt
    masked_suffix = jnp.where(same_request, scores_suffix, -1e+30)
    masked_prefix = jnp.where(prefix_visible, scores_prefix, -1e+30)
    largest = jnp.maximum(lax.optimization_barrier(jnp.max(masked_suffix, 1)), lax.optimization_barrier(jnp.max(masked_prefix, 1)))
    expo_suffix = jnp.where(same_request, jnp.exp(masked_suffix - largest[:, None]), 0.0)
    expo_prefix = jnp.where(prefix_visible, jnp.exp(masked_prefix - largest[:, None]), 0.0)
    denominator = lax.optimization_barrier(jnp.sum(expo_suffix, 1)) + lax.optimization_barrier(jnp.sum(expo_prefix, 1))
    numerator = jnp.dot(expo_suffix.astype(jnp.bfloat16), value_head, preferred_element_type=jnp.float32)
    numerator = numerator + jnp.dot(expo_prefix.astype(jnp.bfloat16), prefix_value, preferred_element_type=jnp.float32)
    return numerator / denominator[:, None]

def reference(queries, suffix_keys, suffix_values, page_cache, page_table, suffix_lengths, request_group, residual, out_weight, attn_gate, mod_shift, mod_scale):
    gathered = page_cache[page_table.reshape(-1)]
    prefix_tokens = GROUPS * PAGES * PAGE
    prefix_key = gathered[:, :, 0, :].reshape(prefix_tokens, HEADS, HS).transpose(1, 0, 2)
    prefix_value = gathered[:, :, 1, :].reshape(prefix_tokens, HEADS, HS).transpose(1, 0, 2)
    prefix_group = jnp.repeat(jnp.arange(GROUPS, dtype=jnp.int32), PAGES * PAGE)

    def block_attention(block):
        query_block, key_block, value_block, lengths_row, groups_row = block
        positions = jnp.arange(TOK_DEV, dtype=jnp.int32)
        request_ends = jnp.cumsum(lengths_row, dtype=jnp.int32)
        request_starts = (request_ends - lengths_row).astype(jnp.int32)
        token_request = lax.optimization_barrier(jnp.sum((positions[:, None] >= request_ends[None, :]).astype(jnp.int32), 1)).astype(jnp.int32)
        choose = token_request[:, None] == jnp.arange(REQ_DEV, dtype=jnp.int32)[None, :]
        token_group = lax.optimization_barrier(jnp.sum(jnp.where(choose, groups_row[None, :], 0), 1)).astype(jnp.int32)
        token_start = lax.optimization_barrier(jnp.sum(jnp.where(choose, request_starts[None, :], 0), 1)).astype(jnp.int32)
        token_block = ((positions - token_start) // SPAN).astype(jnp.int32)
        same_request = (token_request[:, None] == token_request[None, :]) & (token_block[None, :] <= token_block[:, None])
        prefix_visible = token_group[:, None] == prefix_group[None, :]

        def one_head(heads_in):
            query_head, key_head, value_head, key_pre, value_pre = heads_in
            return head_attention(query_head, key_head, value_head, key_pre, value_pre, same_request, prefix_visible)
        outputs = lax.map(one_head, (query_block.transpose(1, 0, 2), key_block.transpose(1, 0, 2), value_block.transpose(1, 0, 2), prefix_key, prefix_value))
        return outputs.transpose(1, 0, 2).reshape(TOK_DEV, HEADS * HS).astype(jnp.bfloat16)
    shaped = (N_REQ, TOK_DEV, HEADS, HS)
    attention = lax.map(block_attention, (queries.reshape(shaped), suffix_keys.reshape(shaped), suffix_values.reshape(shaped), suffix_lengths, request_group))
    attention = attention.reshape(N_REQ * TOK_DEV, HEADS * HS)
    projected = jnp.dot(attention, out_weight, preferred_element_type=jnp.float32)
    combined = residual.astype(jnp.float32) + attn_gate[None, :] * projected
    mean_value = lax.optimization_barrier(jnp.sum(combined, 1)) / D
    variance = lax.optimization_barrier(jnp.sum(combined * combined, 1)) / D - mean_value * mean_value
    normed = (combined - mean_value[:, None]) / jnp.sqrt(variance[:, None] + 1e-06)
    mlp_input = normed * (1.0 + mod_scale[None, :]) + mod_shift[None, :]
    return (combined.astype(jnp.bfloat16), mlp_input.astype(jnp.bfloat16))
```

```python
import functools
import math

import jax
import jax.numpy as jnp
from jax import lax
from jax.experimental import pallas as pl
from jax.experimental.pallas import tpu as pltpu
from jax.sharding import PartitionSpec as P

D = 5120
HS = 128
SPAN = 64
HEADS_DEV = 5
TOK = 256
BIG = -1e30
INV_SQRT = 1.0 / math.sqrt(HS)
EXP2_SCALE = INV_SQRT * math.log2(math.e)


NX, NZ, NC = 4, 4, 2


def rank(x, z, c):
    return ((x % NX) * NZ + z % NZ) * NC + c % NC


def shift(dx, dz, dc):
    return [
        (rank(x, z, c), rank(x + dx, z + dz, c + dc))
        for x in range(NX)
        for z in range(NZ)
        for c in range(NC)
    ]


def token_facts(lens, groups, shape):
    pos = lax.broadcasted_iota(jnp.int32, shape, 0)
    e0 = lens[0]
    e1 = e0 + lens[1]
    e2 = e1 + lens[2]
    after0, after1, after2 = pos >= e0, pos >= e1, pos >= e2
    request = jnp.where(after2, 3, jnp.where(after1, 2, jnp.where(after0, 1, 0)))
    start = jnp.where(after2, e2, jnp.where(after1, e1, jnp.where(after0, e0, 0)))
    group = jnp.where(
        after2, groups[3], jnp.where(after1, groups[2], jnp.where(after0, groups[1], groups[0]))
    )
    block = jnp.where(pos - start >= SPAN, 1, 0)
    return request, block, group


def attend_kernel(own, meta_ref, page_group_ref, q_ref, *refs):
    kv_refs = refs[:8]
    refs = refs[8:]
    if own:
        sk_ref, sv_ref, num_ref, ml_ref, feat, kfeat, scores, ml = refs
    else:
        num_ref, ml_ref, feat, kfeat, scores, ml = refs
    head = pl.program_id(0)
    wide = (TOK, HS)

    @pl.when(head == 0)
    def _():
        lens = [meta_ref[0, i] for i in range(4)]
        groups = [meta_ref[1, i] for i in range(4)]
        request, block, group = token_facts(lens, groups, wide)
        lane = lax.broadcasted_iota(jnp.int32, wide, 1)
        row = lax.broadcasted_iota(jnp.int32, wide, 0)
        feat[0] = jnp.where(lane == group, 1.0, 0.0).astype(jnp.bfloat16)
        for i in range(8):
            page_group = jnp.where(row < 128, page_group_ref[2 * i], page_group_ref[2 * i + 1])
            hidden = (lane < 2) & (lane != page_group)
            kfeat[i] = jnp.where(hidden, BIG, 0.0).astype(jnp.bfloat16)
        if own:
            feat[1] = jnp.where(lane == 2 * request + block, 1.0, 0.0).astype(jnp.bfloat16)
            seen = (request == lane // 2) & (block <= lane % 2)
            kfeat[8] = jnp.where((lane < 8) & ~seen, BIG, 0.0).astype(jnp.bfloat16)
        ml[...] = jnp.zeros_like(ml)

    query = q_ref[...]
    count = 9 if own else 8
    top = None
    for i in range(count):
        key = kv_refs[i][0:TOK, :] if i < 8 else sk_ref[...]
        left = jnp.concatenate([query, feat[0 if i < 8 else 1]], axis=1)
        right = jnp.concatenate([key, kfeat[i]], axis=1)
        score = lax.dot_general(
            left, right, (((1,), (1,)), ((), ())), preferred_element_type=jnp.float32
        )
        scores[:, i * TOK : (i + 1) * TOK] = score
        best = jnp.maximum(score[:, :HS], score[:, HS:])
        top = best if top is None else jnp.maximum(top, best)
    largest = jnp.max(top, axis=1, keepdims=True)
    ones = jnp.ones((TOK, HS), jnp.bfloat16)
    total = None
    for i in range(count):
        value = kv_refs[i][TOK : 2 * TOK, :] if i < 8 else sv_ref[...]
        weight = jnp.exp2((scores[:, i * TOK : (i + 1) * TOK] - largest) * EXP2_SCALE)
        part = jnp.dot(
            weight.astype(jnp.bfloat16),
            jnp.concatenate([value, ones], axis=1),
            preferred_element_type=jnp.float32,
        )
        total = part if total is None else total + part
    num_ref[...] = total[:, :HS].astype(num_ref.dtype)
    lane = lax.broadcasted_iota(jnp.int32, wide, 1)
    ml[...] = jnp.where(lane == head, largest, jnp.where(lane == head + 8, total[:, HS:], ml[...]))

    @pl.when(head == HEADS_DEV - 1)
    def _():
        ml_ref[...] = ml[...].T[0:16, :]


def attend(own, meta, page_group, query, blocks, suffix=()):
    count = 9 if own else 8
    q_spec = pl.BlockSpec((TOK, HS), lambda h, *_: (0, h))
    kv_spec = pl.BlockSpec((2 * TOK, HS), lambda h, *_: (0, h))
    return pl.pallas_call(
        functools.partial(attend_kernel, own),
        name="attend_own" if own else "attend",
        out_shape=(
            jax.ShapeDtypeStruct((TOK, HEADS_DEV * HS), jnp.float32 if own else jnp.bfloat16),
            jax.ShapeDtypeStruct((16, TOK), jnp.float32),
        ),
        grid_spec=pltpu.PrefetchScalarGridSpec(
            num_scalar_prefetch=2,
            grid=(HEADS_DEV,),
            in_specs=[q_spec] + [kv_spec] * 8 + [q_spec] * len(suffix),
            out_specs=(q_spec, pl.BlockSpec((16, TOK), lambda h, *_: (0, 0))),
            scratch_shapes=[
                pltpu.VMEM((2, TOK, HS), jnp.bfloat16),
                pltpu.VMEM((9, TOK, HS), jnp.bfloat16),
                pltpu.VMEM((TOK, count * TOK), jnp.float32),
                pltpu.VMEM((TOK, HS), jnp.float32),
            ],
        ),
        cost_estimate=pl.CostEstimate(
            flops=2 * 2 * TOK * TOK * count * HS * HEADS_DEV,
            bytes_accessed=2 * TOK * HS * HEADS_DEV * (2 * count + 2),
            transcendentals=TOK * TOK * count * HEADS_DEV,
        ),
    )(meta, page_group, query, *blocks, *suffix)


def project_kernel(n0, n1, n2, n3, s0, s1, s2, s3, w_ref, out_ref, att):
    @pl.when(pl.program_id(0) == 0)
    def _():
        stats = []
        for s in (s0, s1, s2, s3):
            padded = jnp.concatenate([s[...], jnp.zeros((112, TOK), jnp.float32)], axis=0)
            stats.append(padded.T)
        for h in range(HEADS_DEV):
            tops = [s[:, h : h + 1] for s in stats]
            sums = [s[:, h + 8 : h + 9] for s in stats]
            best = jnp.maximum(jnp.maximum(tops[0], tops[1]), jnp.maximum(tops[2], tops[3]))
            parts = [jnp.exp2((t - best) * EXP2_SCALE) for t in tops]
            under = sum(p * s for p, s in zip(parts, sums))
            cols = slice(h * HS, (h + 1) * HS)
            over = sum(
                p * n[:, cols].astype(jnp.float32) for p, n in zip(parts, (n0, n1, n2, n3))
            )
            att[:, cols] = (over / under).astype(jnp.bfloat16)

    out_ref[0] = jnp.dot(
        att[...], w_ref[...], preferred_element_type=jnp.float32
    ).astype(jnp.bfloat16)


def project(nums, mls, weight):
    width = HEADS_DEV * HS
    whole = lambda shape: pl.BlockSpec(shape, lambda j: (0, 0))
    return pl.pallas_call(
        project_kernel,
        name="project",
        out_shape=jax.ShapeDtypeStruct((8, TOK, width), jnp.bfloat16),
        grid=(8,),
        in_specs=[whole((TOK, width))] * 4
        + [whole((16, TOK))] * 4
        + [pl.BlockSpec((width, width), lambda j: (0, j))],
        out_specs=pl.BlockSpec((1, TOK, width), lambda j: (j, 0, 0)),
        scratch_shapes=[pltpu.VMEM((TOK, width), jnp.bfloat16)],
        cost_estimate=pl.CostEstimate(
            flops=2 * TOK * width * D,
            bytes_accessed=2 * (width * D + TOK * D) + 3 * 2 * TOK * width,
            transcendentals=TOK * 20,
        ),
    )(*nums, *mls, weight)


def combine_kernel(parts_ref, residual_ref, gate_ref, combined_ref, sums_ref):
    acc = parts_ref[0].astype(jnp.float32)
    for i in range(1, 8):
        acc = acc + parts_ref[i].astype(jnp.float32)
    combined = residual_ref[...].astype(jnp.float32) + gate_ref[...] * acc
    combined_ref[...] = combined
    first = jnp.sum(combined, axis=1, keepdims=True)
    second = jnp.sum(combined * combined, axis=1, keepdims=True)
    lane = lax.broadcasted_iota(jnp.int32, (TOK, HS), 1)
    both = jnp.where(lane == 0, first, jnp.where(lane == 1, second, 0.0))
    rows = both.T[0:8, :]
    for i in range(8):
        sums_ref[i] = rows


def combine(parts, residual, gate):
    width = residual.shape[1]
    return pl.pallas_call(
        combine_kernel,
        name="combine",
        out_shape=(
            jax.ShapeDtypeStruct((TOK, width), jnp.float32),
            jax.ShapeDtypeStruct((8, 8, TOK), jnp.float32),
        ),
    )(parts, residual, gate)


def finish_kernel(combined_ref, sums_ref, shift_ref, scale_ref, stream_ref, mlp_ref):
    total = sums_ref[0]
    for i in range(1, 8):
        total = total + sums_ref[i]
    mean = total[0:1, :] / D
    variance = total[1:2, :] / D - mean * mean
    inverse = 1.0 / jnp.sqrt(variance + 1e-6)
    rows = lax.broadcasted_iota(jnp.int32, (HS, TOK), 0)
    both = jnp.where(rows == 0, mean, jnp.where(rows == 1, inverse, 0.0)).T
    combined = combined_ref[...]
    stream_ref[...] = combined.astype(jnp.bfloat16)
    normed = (combined - both[:, 0:1]) * both[:, 1:2]
    mlp_ref[...] = (normed * (1.0 + scale_ref[...]) + shift_ref[...]).astype(jnp.bfloat16)


def finish(combined, sums, mod_shift, mod_scale):
    shape = jax.ShapeDtypeStruct(combined.shape, jnp.bfloat16)
    return pl.pallas_call(finish_kernel, name="finish", out_shape=(shape, shape))(
        combined, sums, mod_shift, mod_scale
    )


def body(
    queries,
    suffix_keys,
    suffix_values,
    page_cache,
    page_table,
    suffix_lengths,
    request_group,
    residual,
    out_weight,
    attn_gate,
    mod_shift,
    mod_scale,
):
    width = queries.shape[1]
    send = lambda array, dx, dz, dc: lax.ppermute(array, "req", shift(dx, dz, dc))

    meta = jnp.concatenate([suffix_lengths, request_group], axis=0)
    far = [(0, 2, 0), (0, 1, 0), (0, -1, 0)]
    their_meta = [send(meta, *way) for way in far]
    their_query = [send(queries, *way) for way in far]

    pages = page_cache.transpose(2, 0, 1, 3).reshape(2 * TOK, width)
    mine = [pages] + [send(pages, dx, 0, 0) for dx in (2, 1, -1)]
    blocks = mine + [send(array, 0, 0, 1) for array in mine]

    me = lax.axis_index("req")
    x, z, c = me // (NZ * NC), (me // NC) % NZ, me % NC
    owners = jnp.stack(
        [rank((x - dx) % NX, z, (c + dc) % NC) for dc in (0, 1) for dx in (0, 2, 1, -1)]
    )
    slots = (2 * owners[:, None] + jnp.arange(2, dtype=jnp.int32)[None, :]).reshape(16)
    page_group = jnp.sum((page_table[1][None, :] == slots[:, None]).astype(jnp.int32), 1)

    nums, mls = [], []
    for way, query, facts in zip(far, their_query, their_meta):
        num, ml = attend(False, facts, page_group, query, blocks)
        back = (0, -way[1], 0)
        nums.append(send(num, *back))
        mls.append(send(ml, *back))
    num, ml = attend(True, meta, page_group, queries, blocks, (suffix_keys, suffix_values))
    parts = project([num] + nums, [ml] + mls, out_weight)
    parts = lax.all_to_all(parts, "tp", 0, 0, tiled=True)
    combined, sums = combine(parts, residual, attn_gate[None, :])
    sums = lax.all_to_all(sums, "tp", 0, 0, tiled=True)
    return finish(combined, sums, mod_shift[None, :], mod_scale[None, :])


def solution(mesh):
    in_specs = (
        P("req", "tp"),
        P("req", "tp"),
        P("req", "tp"),
        P("req", None, None, "tp"),
        P(),
        P("req", None),
        P("req", None),
        P("req", "tp"),
        P("tp", None),
        P("tp"),
        P("tp"),
        P("tp"),
    )
    out_specs = (P("req", "tp"), P("req", "tp"))
    return jax.shard_map(body, mesh=mesh, in_specs=in_specs, out_specs=out_specs, check_vma=False)
```

```python
import functools
import math

import jax
import jax.numpy as jnp
from jax import lax
from jax.experimental import pallas as pl
from jax.experimental.pallas import tpu as pltpu
from jax.sharding import PartitionSpec as P

D = 5120
HS = 128
SPAN = 64
HEADS_DEV = 5
TOK = 256
BIG = -1e30
INV_SQRT = 1.0 / math.sqrt(HS)
EXP2_SCALE = INV_SQRT * math.log2(math.e)


NX, NZ, NC = 4, 4, 2


def rank(x, z, c):
    return ((x % NX) * NZ + z % NZ) * NC + c % NC


def shift(dx, dz, dc):
    return [
        (rank(x, z, c), rank(x + dx, z + dz, c + dc))
        for x in range(NX)
        for z in range(NZ)
        for c in range(NC)
    ]


def token_facts(lens, groups, shape):
    pos = lax.broadcasted_iota(jnp.int32, shape, 0)
    e0 = lens[0]
    e1 = e0 + lens[1]
    e2 = e1 + lens[2]
    after0, after1, after2 = pos >= e0, pos >= e1, pos >= e2
    request = jnp.where(after2, 3, jnp.where(after1, 2, jnp.where(after0, 1, 0)))
    start = jnp.where(after2, e2, jnp.where(after1, e1, jnp.where(after0, e0, 0)))
    group = jnp.where(
        after2, groups[3], jnp.where(after1, groups[2], jnp.where(after0, groups[1], groups[0]))
    )
    block = jnp.where(pos - start >= SPAN, 1, 0)
    return request, block, group


def attend_kernel(own, meta_ref, page_group_ref, q_ref, *refs):
    kv_refs = refs[:8]
    refs = refs[8:]
    if own:
        sk_ref, sv_ref, num_ref, ml_ref, feat, kfeat, scores, top, ml = refs
    else:
        num_ref, ml_ref, feat, kfeat, scores, top, ml = refs
    head = pl.program_id(0)
    wide = (TOK, HS)

    @pl.when(head == 0)
    def _():
        lens = [meta_ref[0, i] for i in range(4)]
        groups = [meta_ref[1, i] for i in range(4)]
        request, block, group = token_facts(lens, groups, wide)
        lane = lax.broadcasted_iota(jnp.int32, wide, 1)
        row = lax.broadcasted_iota(jnp.int32, wide, 0)
        feat[0] = jnp.where(lane == group, 1.0, 0.0).astype(jnp.bfloat16)
        for i in range(8):
            page_group = jnp.where(row < 128, page_group_ref[2 * i], page_group_ref[2 * i + 1])
            hidden = (lane < 2) & (lane != page_group)
            kfeat[i] = jnp.where(hidden, BIG, 0.0).astype(jnp.bfloat16)
        if own:
            feat[1] = jnp.where(lane == 2 * request + block, 1.0, 0.0).astype(jnp.bfloat16)
            seen = (request == lane // 2) & (block <= lane % 2)
            kfeat[8] = jnp.where((lane < 8) & ~seen, BIG, 0.0).astype(jnp.bfloat16)
        ml[...] = jnp.zeros_like(ml)

    count = 9 if own else 8
    live = meta_ref[0, 0] > 0

    @pl.when(live)
    def _():
        query = q_ref[...]
        best = None
        for i in range(count):
            key = kv_refs[i][0:TOK, :] if i < 8 else sk_ref[...]
            left = jnp.concatenate([query, feat[0 if i < 8 else 1]], axis=1)
            right = jnp.concatenate([key, kfeat[i]], axis=1)
            score = lax.dot_general(
                left, right, (((1,), (1,)), ((), ())), preferred_element_type=jnp.float32
            )
            scores[:, i * TOK : (i + 1) * TOK] = score
            here = jnp.maximum(score[:, :HS], score[:, HS:])
            best = here if best is None else jnp.maximum(best, here)
        top[...] = jnp.broadcast_to(jnp.max(best, axis=1, keepdims=True), wide)

    @pl.when(meta_ref[0, 1] > 0)
    def _():
        largest = top[...]
        both = jnp.concatenate([largest, largest], axis=1)
        ones = jnp.ones((TOK, HS), jnp.bfloat16)
        total = None
        for i in range(count):
            value = kv_refs[i][TOK : 2 * TOK, :] if i < 8 else sv_ref[...]
            weight = jnp.exp2((scores[:, i * TOK : (i + 1) * TOK] - both) * EXP2_SCALE)
            part = jnp.dot(
                weight.astype(jnp.bfloat16),
                jnp.concatenate([value, ones], axis=1),
                preferred_element_type=jnp.float32,
            )
            total = part if total is None else total + part
        num_ref[...] = total[:, :HS].astype(num_ref.dtype)
        lane = lax.broadcasted_iota(jnp.int32, wide, 1)
        ml[...] = jnp.where(
            lane == head, largest, jnp.where(lane == head + 8, total[:, HS:], ml[...])
        )

    @pl.when(head == HEADS_DEV - 1)
    def _():
        ml_ref[...] = ml[...].T[0:16, :]


def attend(own, meta, page_group, query, blocks, suffix=()):
    count = 9 if own else 8
    q_spec = pl.BlockSpec((TOK, HS), lambda h, *_: (0, h))
    kv_spec = pl.BlockSpec((2 * TOK, HS), lambda h, *_: (0, h))
    return pl.pallas_call(
        functools.partial(attend_kernel, own),
        name="attend_own" if own else "attend",
        out_shape=(
            jax.ShapeDtypeStruct((TOK, HEADS_DEV * HS), jnp.float32 if own else jnp.bfloat16),
            jax.ShapeDtypeStruct((16, TOK), jnp.float32),
        ),
        grid_spec=pltpu.PrefetchScalarGridSpec(
            num_scalar_prefetch=2,
            grid=(HEADS_DEV,),
            in_specs=[q_spec] + [kv_spec] * 8 + [q_spec] * len(suffix),
            out_specs=(q_spec, pl.BlockSpec((16, TOK), lambda h, *_: (0, 0))),
            scratch_shapes=[
                pltpu.VMEM((2, TOK, HS), jnp.bfloat16),
                pltpu.VMEM((9, TOK, HS), jnp.bfloat16),
                pltpu.VMEM((TOK, count * TOK), jnp.float32),
                pltpu.VMEM((TOK, HS), jnp.float32),
                pltpu.VMEM((TOK, HS), jnp.float32),
            ],
        ),
        cost_estimate=pl.CostEstimate(
            flops=2 * 2 * TOK * TOK * count * HS * HEADS_DEV,
            bytes_accessed=2 * TOK * HS * HEADS_DEV * (2 * count + 2),
            transcendentals=TOK * TOK * count * HEADS_DEV,
        ),
    )(meta, page_group, query, *blocks, *suffix)


def project_kernel(n0, n1, n2, n3, s0, s1, s2, s3, w_ref, out_ref, att):
    @pl.when(pl.program_id(0) == 0)
    def _():
        tops = [s[0:8, :] for s in (s0, s1, s2, s3)]
        sums = [s[8:16, :] for s in (s0, s1, s2, s3)]
        best = jnp.maximum(jnp.maximum(tops[0], tops[1]), jnp.maximum(tops[2], tops[3]))
        parts = [jnp.exp2((t - best) * EXP2_SCALE) for t in tops]
        under = sum(p * s for p, s in zip(parts, sums))
        rows = [p / under for p in parts] + [jnp.zeros((96, TOK), jnp.float32)]
        share = jnp.concatenate(rows, axis=0).T
        for h in range(HEADS_DEV):
            cols = slice(h * HS, (h + 1) * HS)
            merged = sum(
                share[:, 8 * i + h : 8 * i + h + 1] * n[:, cols].astype(jnp.float32)
                for i, n in enumerate((n0, n1, n2, n3))
            )
            att[:, cols] = merged.astype(jnp.bfloat16)

    width = HEADS_DEV * HS
    done = jnp.dot(att[...], w_ref[...], preferred_element_type=jnp.float32)
    out_ref[0] = done[:, :width].astype(jnp.bfloat16)
    out_ref[1] = done[:, width:].astype(jnp.bfloat16)


def project(nums, mls, weight):
    width = HEADS_DEV * HS
    whole = lambda shape: pl.BlockSpec(shape, lambda j: (0, 0))
    return pl.pallas_call(
        project_kernel,
        name="project",
        out_shape=jax.ShapeDtypeStruct((8, TOK, width), jnp.bfloat16),
        grid=(4,),
        in_specs=[whole((TOK, width))] * 4
        + [whole((16, TOK))] * 4
        + [pl.BlockSpec((width, 2 * width), lambda j: (0, j))],
        out_specs=pl.BlockSpec((2, TOK, width), lambda j: (j, 0, 0)),
        scratch_shapes=[pltpu.VMEM((TOK, width), jnp.bfloat16)],
        cost_estimate=pl.CostEstimate(
            flops=2 * TOK * width * D,
            bytes_accessed=2 * (width * D + TOK * D) + 3 * 2 * TOK * width,
            transcendentals=TOK * 20,
        ),
    )(*nums, *mls, weight)


def combine_kernel(parts_ref, residual_ref, gate_ref, combined_ref, sums_ref):
    acc = parts_ref[0].astype(jnp.float32)
    for i in range(1, 8):
        acc = acc + parts_ref[i].astype(jnp.float32)
    combined = residual_ref[...].astype(jnp.float32) + gate_ref[...] * acc
    combined_ref[...] = combined
    first = jnp.sum(combined, axis=1, keepdims=True)
    second = jnp.sum(combined * combined, axis=1, keepdims=True)
    lane = lax.broadcasted_iota(jnp.int32, (HS, HS), 1)
    both = jnp.where(lane == 0, first, jnp.where(lane == 1, second, 0.0))
    rows = both.T[0:8, :]
    for i in range(8):
        sums_ref[i] = rows


def combine(parts, residual, gate):
    width = residual.shape[1]
    return pl.pallas_call(
        combine_kernel,
        name="combine",
        grid=(TOK // HS,),
        in_specs=[
            pl.BlockSpec((8, HS, width), lambda i: (0, i, 0)),
            pl.BlockSpec((HS, width), lambda i: (i, 0)),
            pl.BlockSpec((1, width), lambda i: (0, 0)),
        ],
        out_specs=(
            pl.BlockSpec((HS, width), lambda i: (i, 0)),
            pl.BlockSpec((8, 8, HS), lambda i: (0, 0, i)),
        ),
        out_shape=(
            jax.ShapeDtypeStruct((TOK, width), jnp.float32),
            jax.ShapeDtypeStruct((8, 8, TOK), jnp.float32),
        ),
    )(parts, residual, gate)


def finish_kernel(combined_ref, sums_ref, shift_ref, scale_ref, stream_ref, mlp_ref):
    total = sums_ref[0]
    for i in range(1, 8):
        total = total + sums_ref[i]
    mean = total[0:1, :] / D
    variance = total[1:2, :] / D - mean * mean
    inverse = 1.0 / jnp.sqrt(variance + 1e-6)
    rows = lax.broadcasted_iota(jnp.int32, (HS, TOK), 0)
    both = jnp.where(rows == 0, mean, jnp.where(rows == 1, inverse, 0.0)).T
    combined = combined_ref[...]
    stream_ref[...] = combined.astype(jnp.bfloat16)
    normed = (combined - both[:, 0:1]) * both[:, 1:2]
    mlp_ref[...] = (normed * (1.0 + scale_ref[...]) + shift_ref[...]).astype(jnp.bfloat16)


def finish(combined, sums, mod_shift, mod_scale):
    shape = jax.ShapeDtypeStruct(combined.shape, jnp.bfloat16)
    return pl.pallas_call(finish_kernel, name="finish", out_shape=(shape, shape))(
        combined, sums, mod_shift, mod_scale
    )


def body(
    queries,
    suffix_keys,
    suffix_values,
    page_cache,
    page_table,
    suffix_lengths,
    request_group,
    residual,
    out_weight,
    attn_gate,
    mod_shift,
    mod_scale,
):
    width = queries.shape[1]
    send = lambda array, dx, dz, dc: lax.ppermute(array, "req", shift(dx, dz, dc))

    meta = jnp.concatenate([suffix_lengths, request_group], axis=0)
    far = [(0, 2, 0), (0, 1, 0), (0, -1, 0)]
    their_meta = [send(meta, *way) for way in far]
    their_query = [send(queries, *way) for way in far]

    pages = page_cache.transpose(2, 0, 1, 3).reshape(2 * TOK, width)
    mine = [pages] + [send(pages, dx, 0, 0) for dx in (2, 1, -1)]
    blocks = mine + [send(array, 0, 0, 1) for array in mine]

    me = lax.axis_index("req")
    x, z, c = me // (NZ * NC), (me // NC) % NZ, me % NC
    owners = jnp.stack(
        [rank((x - dx) % NX, z, (c + dc) % NC) for dc in (0, 1) for dx in (0, 2, 1, -1)]
    )
    slots = (2 * owners[:, None] + jnp.arange(2, dtype=jnp.int32)[None, :]).reshape(16)
    page_group = jnp.sum((page_table[1][None, :] == slots[:, None]).astype(jnp.int32), 1)

    nums, mls = [], []
    for way, query, facts in zip(far, their_query, their_meta):
        num, ml = attend(False, facts, page_group, query, blocks)
        back = (0, -way[1], 0)
        nums.append(send(num, *back))
        mls.append(send(ml, *back))
    num, ml = attend(True, meta, page_group, queries, blocks, (suffix_keys, suffix_values))
    parts = project([num] + nums, [ml] + mls, out_weight)
    parts = lax.all_to_all(parts, "tp", 0, 0, tiled=True)
    combined, sums = combine(parts, residual, attn_gate[None, :])
    sums = lax.all_to_all(sums, "tp", 0, 0, tiled=True)
    return finish(combined, sums, mod_shift[None, :], mod_scale[None, :])


def solution(mesh):
    in_specs = (
        P("req", "tp"),
        P("req", "tp"),
        P("req", "tp"),
        P("req", None, None, "tp"),
        P(),
        P("req", None),
        P("req", None),
        P("req", "tp"),
        P("tp", None),
        P("tp"),
        P("tp"),
        P("tp"),
    )
    out_specs = (P("req", "tp"), P("req", "tp"))
    return jax.shard_map(body, mesh=mesh, in_specs=in_specs, out_specs=out_specs, check_vma=False)
```

```python
import functools
import math

import jax
import jax.numpy as jnp
from jax import lax
from jax.experimental import pallas as pl
from jax.experimental.pallas import tpu as pltpu
from jax.sharding import PartitionSpec as P


D = 5120
HS = 128
SPAN = 64
HEADS_DEV = 5
TOK = 256
BIG = -1e30
INV_SQRT = 1.0 / math.sqrt(HS)
EXP2_SCALE = INV_SQRT * math.log2(math.e)


NX, NZ, NC = 4, 4, 2


def rank(x, z, c):
    return ((x % NX) * NZ + z % NZ) * NC + c % NC


def shift(dx, dz, dc):
    return [
        (rank(x, z, c), rank(x + dx, z + dz, c + dc))
        for x in range(NX)
        for z in range(NZ)
        for c in range(NC)
    ]


def token_facts(facts, shape):
    lane = lax.broadcasted_iota(jnp.int32, facts.shape, 1)
    pick = lambda j: jnp.sum(jnp.where(lane == j, facts, 0.0), axis=1, keepdims=True)
    lens = [pick(j).astype(jnp.int32) for j in range(3)]
    groups = [pick(4 + j).astype(jnp.int32) for j in range(4)]
    pos = lax.broadcasted_iota(jnp.int32, shape, 0)
    e0 = lens[0]
    e1 = e0 + lens[1]
    e2 = e1 + lens[2]
    after0, after1, after2 = pos >= e0, pos >= e1, pos >= e2
    request = jnp.where(after2, 3, jnp.where(after1, 2, jnp.where(after0, 1, 0)))
    start = jnp.where(after2, e2, jnp.where(after1, e1, jnp.where(after0, e0, 0)))
    group = jnp.where(
        after2, groups[3], jnp.where(after1, groups[2], jnp.where(after0, groups[1], groups[0]))
    )
    block = jnp.where(pos - start >= SPAN, 1, 0)
    return request, block, group


def features(own, first, page_group_ref, q_ref, feat, kfeat, blocks):
    wide = (TOK, HS)
    facts = q_ref[TOK : TOK + 16, :].astype(jnp.float32)[0:1, :]
    request, block, group = token_facts(facts, wide)
    lane = lax.broadcasted_iota(jnp.int32, wide, 1)
    row = lax.broadcasted_iota(jnp.int32, wide, 0)
    feat[0] = jnp.where(lane == group, 1.0, 0.0).astype(jnp.bfloat16)
    for i in range(blocks):
        low, high = page_group_ref[first + 2 * i], page_group_ref[first + 2 * i + 1]
        hidden = (lane < 2) & (lane != jnp.where(row < 128, low, high))
        kfeat[i] = jnp.where(hidden, BIG, 0.0).astype(jnp.bfloat16)
    if own:
        feat[1] = jnp.where(lane == 2 * request + block, 1.0, 0.0).astype(jnp.bfloat16)
        seen = (request == lane // 2) & (block <= lane % 2)
        kfeat[blocks] = jnp.where((lane < 8) & ~seen, BIG, 0.0).astype(jnp.bfloat16)


def score_pass(query, keys, marks, feat, kfeat, scores, floor):
    best = floor
    for i, (key, mark) in enumerate(zip(keys, marks)):
        left = jnp.concatenate([query, feat[mark]], axis=1)
        right = jnp.concatenate([key, kfeat[i]], axis=1)
        score = lax.dot_general(
            left, right, (((1,), (1,)), ((), ())), preferred_element_type=jnp.float32
        )
        scores[:, i * TOK : (i + 1) * TOK] = score
        here = jnp.maximum(score[:, :HS], score[:, HS:])
        best = here if best is None else jnp.maximum(best, here)
    return jnp.broadcast_to(jnp.max(best, axis=1, keepdims=True), (TOK, HS))


def value_pass(values, scores, largest):
    both = jnp.concatenate([largest, largest], axis=1)
    ones = jnp.ones((TOK, HS), jnp.bfloat16)
    total = None
    for i, value in enumerate(values):
        weight = jnp.exp2((scores[:, i * TOK : (i + 1) * TOK] - both) * EXP2_SCALE)
        part = jnp.dot(
            weight.astype(jnp.bfloat16),
            jnp.concatenate([value, ones], axis=1),
            preferred_element_type=jnp.float32,
        )
        total = part if total is None else total + part
    return total[:, :HS], total[:, HS:]


def near_kernel(own, page_group_ref, q_ref, *refs):
    kv_refs, refs = refs[:6], refs[6:]
    suffix, refs = (refs[:2], refs[2:]) if own else ((), refs)
    num_ref, top_ref, sum_ref, feat, kfeat, scores = refs

    @pl.when(pl.program_id(0) == 0)
    def _():
        features(own, 0, page_group_ref, q_ref, feat, kfeat, 6)

    @pl.when(page_group_ref[0] >= 0)
    def _():
        keys = [jnp.concatenate([r[0:128, :], r[256:384, :]], axis=0) for r in kv_refs]
        keys = keys + [r[...] for r in suffix[:1]]
        marks = [0] * 6 + [1]
        top_ref[...] = score_pass(q_ref[0:TOK, :], keys, marks, feat, kfeat, scores, None)

    @pl.when(page_group_ref[1] >= 0)
    def _():
        values = [jnp.concatenate([r[128:256, :], r[384:512, :]], axis=0) for r in kv_refs]
        values = values + [r[...] for r in suffix[1:]]
        num_ref[...], sum_ref[...] = value_pass(values, scores, top_ref[...])


def near(own, page_group, query, blocks, suffix=()):
    count = 7 if own else 6
    q_spec = pl.BlockSpec((TOK + 16, HS), lambda h, *_: (0, h))
    s_spec = pl.BlockSpec((TOK, HS), lambda h, *_: (0, h))
    kv_spec = pl.BlockSpec((2 * TOK, HS), lambda h, *_: (0, h))
    out = jax.ShapeDtypeStruct((TOK, HEADS_DEV * HS), jnp.float32)
    return pl.pallas_call(
        functools.partial(near_kernel, own),
        name="near_own" if own else "near",
        out_shape=(out, out, out),
        grid_spec=pltpu.PrefetchScalarGridSpec(
            num_scalar_prefetch=1,
            grid=(HEADS_DEV,),
            in_specs=[q_spec]
            + [kv_spec] * 6
            + [s_spec] * len(suffix),
            out_specs=(s_spec, s_spec, s_spec),
            scratch_shapes=[
                pltpu.VMEM((2, TOK, HS), jnp.bfloat16),
                pltpu.VMEM((7, TOK, HS), jnp.bfloat16),
                pltpu.VMEM((TOK, count * TOK), jnp.float32),
            ],
        ),
        compiler_params=pltpu.CompilerParams(vmem_limit_bytes=24 << 20),
        cost_estimate=pl.CostEstimate(
            flops=2 * 2 * TOK * TOK * count * HS * HEADS_DEV,
            bytes_accessed=2 * TOK * HS * HEADS_DEV * (2 * count + 7),
            transcendentals=TOK * TOK * count * HEADS_DEV,
        ),
    )(page_group, query, *blocks, *suffix)


def far_kernel(own, page_group_ref, q_ref, u0, v0, u1, v1, num_in, top_in, sum_in, *refs):
    if own:
        num_ref, ml_ref, feat, kfeat, scores, top, ml = refs
    else:
        num_ref, feat, kfeat, scores, top, ml = refs
    head = pl.program_id(0)
    wide = (TOK, HS)

    @pl.when(head == 0)
    def _():
        features(False, 12, page_group_ref, q_ref, feat, kfeat, 2)
        ml[...] = jnp.zeros_like(ml)

    @pl.when(page_group_ref[0] >= 0)
    def _():
        keys = [jnp.concatenate([a[0:128, :], b[0:128, :]], axis=0) for a, b in ((u0, v0), (u1, v1))]
        top[...] = score_pass(q_ref[0:TOK, :], keys, [0, 0], feat, kfeat, scores, top_in[...])

    @pl.when(page_group_ref[1] >= 0)
    def _():
        largest = top[...]
        values = [
            jnp.concatenate([a[128:256, :], b[128:256, :]], axis=0) for a, b in ((u0, v0), (u1, v1))
        ]
        num, total = value_pass(values, scores, largest)
        keep = jnp.exp2((top_in[...] - largest) * EXP2_SCALE)
        num = num + keep * num_in[...]
        total = total + keep * sum_in[...]
        if own:
            num_ref[...] = num
        else:
            cols = pl.ds(pl.multiple_of(head * HS, HS), HS)
            num_ref[0:TOK, cols] = num.astype(jnp.bfloat16)
        lane = lax.broadcasted_iota(jnp.int32, wide, 1)
        ml[...] = jnp.where(lane == head, largest, jnp.where(lane == head + 8, total, ml[...]))

    @pl.when(head == HEADS_DEV - 1)
    def _():
        rows = ml[...].T[0:16, :]
        if own:
            ml_ref[...] = rows
        else:
            high = rows.astype(jnp.bfloat16)
            rest = rows - high.astype(jnp.float32)
            middle = rest.astype(jnp.bfloat16)
            low = (rest - middle.astype(jnp.float32))[0:8, :]
            low = jnp.concatenate([low[:, 0:HS], low[:, HS:]], axis=0).astype(jnp.bfloat16)
            num_ref[TOK : TOK + 16, :] = jnp.concatenate([high, middle, low], axis=1)


def far(own, page_group, query, blocks, state):
    width = HEADS_DEV * HS
    q_spec = pl.BlockSpec((TOK + 16, HS), lambda h, *_: (0, h))
    s_spec = pl.BlockSpec((TOK, HS), lambda h, *_: (0, h))
    if own:
        out_shape = (
            jax.ShapeDtypeStruct((TOK, width), jnp.float32),
            jax.ShapeDtypeStruct((16, TOK), jnp.float32),
        )
        out_specs = (s_spec, pl.BlockSpec((16, TOK), lambda h, *_: (0, 0)))
    else:
        out_shape = jax.ShapeDtypeStruct((TOK + 16, width), jnp.bfloat16)
        out_specs = pl.BlockSpec((TOK + 16, width), lambda h, *_: (0, 0))
    return pl.pallas_call(
        functools.partial(far_kernel, own),
        name="far_own" if own else "far",
        out_shape=out_shape,
        grid_spec=pltpu.PrefetchScalarGridSpec(
            num_scalar_prefetch=1,
            grid=(HEADS_DEV,),
            in_specs=[q_spec] + [s_spec] * 7,
            out_specs=out_specs,
            scratch_shapes=[
                pltpu.VMEM((2, TOK, HS), jnp.bfloat16),
                pltpu.VMEM((2, TOK, HS), jnp.bfloat16),
                pltpu.VMEM((TOK, 2 * TOK), jnp.float32),
                pltpu.VMEM((TOK, HS), jnp.float32),
                pltpu.VMEM((TOK, HS), jnp.float32),
            ],
        ),
        compiler_params=pltpu.CompilerParams(vmem_limit_bytes=24 << 20),
        cost_estimate=pl.CostEstimate(
            flops=2 * 2 * TOK * TOK * 2 * HS * HEADS_DEV,
            bytes_accessed=2 * TOK * HS * HEADS_DEV * 12,
            transcendentals=TOK * TOK * 2 * HEADS_DEV,
        ),
    )(page_group, query, *blocks, *state)


def project_kernel(n0, s0, n1, n2, n3, w_ref, out_ref, att):
    @pl.when(pl.program_id(0) == 0)
    def _():
        tops, sums = [s0[0:8, :]], [s0[8:16, :]]
        for n in (n1, n2, n3):
            piece = n[TOK : TOK + 16, :].astype(jnp.float32)
            low = jnp.concatenate([piece[0:8, 2 * TOK :], piece[8:16, 2 * TOK :]], axis=1)
            tops.append(piece[0:8, :TOK] + piece[0:8, TOK : 2 * TOK] + low)
            sums.append(piece[8:16, :TOK] + piece[8:16, TOK : 2 * TOK])
        best = jnp.maximum(jnp.maximum(tops[0], tops[1]), jnp.maximum(tops[2], tops[3]))
        parts = [jnp.exp2((t - best) * EXP2_SCALE) for t in tops]
        under = sum(p * s for p, s in zip(parts, sums))
        rows = [p / under for p in parts] + [jnp.zeros((96, TOK), jnp.float32)]
        share = jnp.concatenate(rows, axis=0).T
        for h in range(HEADS_DEV):
            cols = slice(h * HS, (h + 1) * HS)
            merged = sum(
                share[:, 8 * i + h : 8 * i + h + 1] * n[0:TOK, cols].astype(jnp.float32)
                for i, n in enumerate((n0, n1, n2, n3))
            )
            att[:, cols] = merged.astype(jnp.bfloat16)

    width = HEADS_DEV * HS
    done = jnp.dot(att[...], w_ref[...], preferred_element_type=jnp.float32)
    out_ref[0] = done[:, :width].astype(jnp.bfloat16)
    out_ref[1] = done[:, width:].astype(jnp.bfloat16)


def project(num, ml, others, weight):
    width = HEADS_DEV * HS
    whole = lambda shape: pl.BlockSpec(shape, lambda j: (0, 0))
    return pl.pallas_call(
        project_kernel,
        name="project",
        out_shape=jax.ShapeDtypeStruct((8, TOK, width), jnp.bfloat16),
        grid=(4,),
        in_specs=[whole((TOK, width)), whole((16, TOK))]
        + [whole((TOK + 16, width))] * 3
        + [pl.BlockSpec((width, 2 * width), lambda j: (0, j))],
        out_specs=pl.BlockSpec((2, TOK, width), lambda j: (j, 0, 0)),
        scratch_shapes=[pltpu.VMEM((TOK, width), jnp.bfloat16)],
        cost_estimate=pl.CostEstimate(
            flops=2 * TOK * width * D,
            bytes_accessed=2 * (width * D + TOK * D) + 3 * 2 * TOK * width,
            transcendentals=TOK * 20,
        ),
    )(num, ml, *others, weight)


def combine_kernel(parts_ref, residual_ref, gate_ref, combined_ref, sums_ref):
    acc = parts_ref[0].astype(jnp.float32)
    for i in range(1, 8):
        acc = acc + parts_ref[i].astype(jnp.float32)
    combined = residual_ref[...].astype(jnp.float32) + gate_ref[...] * acc
    combined_ref[...] = combined
    first = jnp.sum(combined, axis=1, keepdims=True)
    second = jnp.sum(combined * combined, axis=1, keepdims=True)
    lane = lax.broadcasted_iota(jnp.int32, (HS, HS), 1)
    both = jnp.where(lane == 0, first, jnp.where(lane == 1, second, 0.0))
    rows = both.T[0:8, :]
    for i in range(8):
        sums_ref[i] = rows


def combine(parts, residual, gate):
    width = residual.shape[1]
    return pl.pallas_call(
        combine_kernel,
        name="combine",
        grid=(TOK // HS,),
        in_specs=[
            pl.BlockSpec((8, HS, width), lambda i: (0, i, 0)),
            pl.BlockSpec((HS, width), lambda i: (i, 0)),
            pl.BlockSpec((1, width), lambda i: (0, 0)),
        ],
        out_specs=(
            pl.BlockSpec((HS, width), lambda i: (i, 0)),
            pl.BlockSpec((8, 8, HS), lambda i: (0, 0, i)),
        ),
        out_shape=(
            jax.ShapeDtypeStruct((TOK, width), jnp.float32),
            jax.ShapeDtypeStruct((8, 8, TOK), jnp.float32),
        ),
    )(parts, residual, gate)


def finish_kernel(combined_ref, sums_ref, shift_ref, scale_ref, stream_ref, mlp_ref):
    total = sums_ref[0]
    for i in range(1, 8):
        total = total + sums_ref[i]
    mean = total[0:1, :] / D
    variance = total[1:2, :] / D - mean * mean
    inverse = 1.0 / jnp.sqrt(variance + 1e-6)
    rows = lax.broadcasted_iota(jnp.int32, (HS, TOK), 0)
    both = jnp.where(rows == 0, mean, jnp.where(rows == 1, inverse, 0.0)).T
    combined = combined_ref[...]
    stream_ref[...] = combined.astype(jnp.bfloat16)
    normed = (combined - both[:, 0:1]) * both[:, 1:2]
    mlp_ref[...] = (normed * (1.0 + scale_ref[...]) + shift_ref[...]).astype(jnp.bfloat16)


def finish(combined, sums, mod_shift, mod_scale):
    shape = jax.ShapeDtypeStruct(combined.shape, jnp.bfloat16)
    return pl.pallas_call(finish_kernel, name="finish", out_shape=(shape, shape))(
        combined, sums, mod_shift, mod_scale
    )


def body(
    queries,
    suffix_keys,
    suffix_values,
    page_cache,
    page_table,
    suffix_lengths,
    request_group,
    residual,
    out_weight,
    attn_gate,
    mod_shift,
    mod_scale,
):
    width = queries.shape[1]
    send = lambda array, dx, dz, dc: lax.ppermute(array, "req", shift(dx, dz, dc))

    facts = jnp.concatenate([suffix_lengths, request_group], axis=1).astype(jnp.bfloat16)
    query = jnp.concatenate([queries, jnp.pad(facts, ((0, 15), (0, width - 8)))], axis=0)
    ways = [1, -1, 2]
    their_query = []
    for dz in ways:
        their_query.append(send(query, 0, dz, 0))

    pages = page_cache.transpose(0, 2, 1, 3).reshape(2 * TOK, width)
    left, right = send(pages, 1, 0, 0), send(pages, -1, 0, 0)
    over_left = send(left[:TOK], 1, 0, 0)
    over_right = send(right[TOK:], -1, 0, 0)
    near_blocks = [pages, left, right]
    near_blocks = near_blocks + [send(array, 0, 0, 1) for array in near_blocks]
    far_blocks = [over_left, over_right]
    far_blocks.append(send(over_left, 0, 0, 1))
    far_blocks.append(send(over_right, 0, 0, 1))

    me = lax.axis_index("req")
    x, z, c = me // (NZ * NC), (me // NC) % NZ, me % NC
    owners = jnp.stack(
        [rank(x - dx, z, c + dc) for dc in (0, 1) for dx in (0, 1, -1)]
        + [rank(x + 2, z, c), rank(x + 2, z, c + 1)]
    )
    slots = (2 * owners[:, None] + jnp.arange(2, dtype=jnp.int32)[None, :]).reshape(16)
    page_group = jnp.sum((page_table[1][None, :] == slots[:, None]).astype(jnp.int32), 1)

    suffix = (suffix_keys, suffix_values)
    states, others = [], []
    for q in their_query:
        states.append(near(False, page_group, q, near_blocks))
    for q, state, dz in zip(their_query, states, ways):
        num = far(False, page_group, q, far_blocks, state)
        others.append(send(num, 0, -dz, 0))
    state = near(True, page_group, query, near_blocks, suffix)
    num, ml = far(True, page_group, query, far_blocks, state)
    parts = project(num, ml, others, out_weight)
    parts = lax.all_to_all(parts, "tp", 0, 0, tiled=True)
    combined, sums = combine(parts, residual, attn_gate[None, :])
    sums = lax.all_to_all(sums, "tp", 0, 0, tiled=True)
    return finish(combined, sums, mod_shift[None, :], mod_scale[None, :])


def solution(mesh):
    in_specs = (
        P("req", "tp"),
        P("req", "tp"),
        P("req", "tp"),
        P("req", None, None, "tp"),
        P(),
        P("req", None),
        P("req", None),
        P("req", "tp"),
        P("tp", None),
        P("tp"),
        P("tp"),
        P("tp"),
    )
    out_specs = (P("req", "tp"), P("req", "tp"))

    return jax.shard_map(body, mesh=mesh, in_specs=in_specs, out_specs=out_specs, check_vma=False)
```

```python
import functools
import math

import jax
import jax.numpy as jnp
from jax import lax
from jax.experimental import pallas as pl
from jax.experimental.pallas import tpu as pltpu
from jax.sharding import PartitionSpec as P


D = 5120
HS = 128
SPAN = 64
HEADS_DEV = 5
TOK = 256
BIG = -1e30
INV_SQRT = 1.0 / math.sqrt(HS)
EXP2_SCALE = INV_SQRT * math.log2(math.e)


NX, NZ, NC = 4, 4, 2


def rank(x, z, c):
    return ((x % NX) * NZ + z % NZ) * NC + c % NC


def shift(dx, dz, dc):
    return [
        (rank(x, z, c), rank(x + dx, z + dz, c + dc))
        for x in range(NX)
        for z in range(NZ)
        for c in range(NC)
    ]


def token_facts(facts, shape):
    lane = lax.broadcasted_iota(jnp.int32, facts.shape, 1)
    pick = lambda j: jnp.sum(jnp.where(lane == j, facts, 0.0), axis=1, keepdims=True)
    lens = [pick(j).astype(jnp.int32) for j in range(3)]
    groups = [pick(4 + j).astype(jnp.int32) for j in range(4)]
    pos = lax.broadcasted_iota(jnp.int32, shape, 0)
    e0 = lens[0]
    e1 = e0 + lens[1]
    e2 = e1 + lens[2]
    after0, after1, after2 = pos >= e0, pos >= e1, pos >= e2
    request = jnp.where(after2, 3, jnp.where(after1, 2, jnp.where(after0, 1, 0)))
    start = jnp.where(after2, e2, jnp.where(after1, e1, jnp.where(after0, e0, 0)))
    group = jnp.where(
        after2, groups[3], jnp.where(after1, groups[2], jnp.where(after0, groups[1], groups[0]))
    )
    block = jnp.where(pos - start >= SPAN, 1, 0)
    return request, block, group


def pack_kernel(lens_ref, groups_ref, q_ref, out_ref):
    width = q_ref.shape[1]
    out_ref[0:TOK, :] = q_ref[...]
    lane = lax.broadcasted_iota(jnp.int32, (16, width), 1)
    facts = jnp.zeros((16, width), jnp.int32)
    for i in range(4):
        facts = jnp.where(lane == i, lens_ref[0, i], facts)
        facts = jnp.where(lane == 4 + i, groups_ref[0, i], facts)
    out_ref[TOK : TOK + 16, :] = facts.astype(jnp.float32).astype(jnp.bfloat16)


def pack(lens, groups, queries):
    smem = pl.BlockSpec(memory_space=pltpu.SMEM)
    return pl.pallas_call(
        pack_kernel,
        name="pack",
        in_specs=[smem, smem, pl.BlockSpec(memory_space=pltpu.VMEM)],
        out_specs=pl.BlockSpec(memory_space=pltpu.VMEM),
        out_shape=jax.ShapeDtypeStruct((TOK + 16, queries.shape[1]), queries.dtype),
        compiler_params=pltpu.CompilerParams(vmem_limit_bytes=8 << 20),
    )(lens, groups, queries)


def features(own, facts, page_group_ref, feat, kfeat):
    wide = (TOK, HS)
    request, block, group = token_facts(facts.astype(jnp.float32)[0:1, :], wide)
    lane = lax.broadcasted_iota(jnp.int32, wide, 1)
    row = lax.broadcasted_iota(jnp.int32, wide, 0)
    feat[0] = jnp.where(lane == group, 1.0, 0.0).astype(jnp.bfloat16)
    for i in range(8):
        low, high = page_group_ref[2 * i], page_group_ref[2 * i + 1]
        hidden = (lane < 2) & (lane != jnp.where(row < 128, low, high))
        kfeat[i] = jnp.where(hidden, BIG, 0.0).astype(jnp.bfloat16)
    if own:
        feat[1] = jnp.where(lane == 2 * request + block, 1.0, 0.0).astype(jnp.bfloat16)
        seen = (request == lane // 2) & (block <= lane % 2)
        kfeat[8] = jnp.where((lane < 8) & ~seen, BIG, 0.0).astype(jnp.bfloat16)


def score_pass(query, keys, marks, feat, kfeat, scores):
    best = None
    for i, (key, mark) in enumerate(zip(keys, marks)):
        left = jnp.concatenate([query, feat[mark]], axis=1)
        right = jnp.concatenate([key, kfeat[i]], axis=1)
        score = lax.dot_general(
            left, right, (((1,), (1,)), ((), ())), preferred_element_type=jnp.float32
        )
        scores[:, i * TOK : (i + 1) * TOK] = score
        here = jnp.maximum(score[:, :HS], score[:, HS:])
        best = here if best is None else jnp.maximum(best, here)
    return jnp.broadcast_to(jnp.max(best, axis=1, keepdims=True), (TOK, HS))


def value_pass(values, scores, largest):
    both = jnp.concatenate([largest, largest], axis=1)
    ones = jnp.ones((TOK, HS), jnp.bfloat16)
    total = None
    for i, value in enumerate(values):
        weight = jnp.exp2((scores[:, i * TOK : (i + 1) * TOK] - both) * EXP2_SCALE)
        part = jnp.dot(
            weight.astype(jnp.bfloat16),
            jnp.concatenate([value, ones], axis=1),
            preferred_element_type=jnp.float32,
        )
        total = part if total is None else total + part
    return total[:, :HS], total[:, HS:]


def attend_kernel(own, pieces, page_group_ref, *refs):
    q_refs, refs = refs[:pieces], refs[pieces:]
    kv_refs, refs = refs[:10], refs[10:]
    suffix, refs = (refs[:2], refs[2:]) if own else ((), refs)
    if own:
        num_ref, ml_ref, feat, kfeat, scores, top, ml = refs
    else:
        num_ref, feat, kfeat, scores, top, ml = refs
    head = pl.program_id(0)
    wide = (TOK, HS)

    @pl.when(head == 0)
    def _():
        facts = q_refs[-1][TOK // pieces : TOK // pieces + 16, :]
        features(own, facts, page_group_ref, feat, kfeat)
        ml[...] = jnp.zeros_like(ml)

    def rows(start):
        pick = slice(start, start + 128)
        later = slice(start + 256, start + 384)
        out = [jnp.concatenate([r[pick, :], r[later, :]], axis=0) for r in kv_refs[:6]]
        for a, b in (kv_refs[6:8], kv_refs[8:10]):
            out.append(jnp.concatenate([a[pick, :], b[pick, :]], axis=0))
        return out

    @pl.when(page_group_ref[0] >= 0)
    def _():
        if pieces == 1:
            query = q_refs[0][0:TOK, :]
        else:
            query = jnp.concatenate([q_refs[0][...], q_refs[1][0:128, :]], axis=0)
        keys = rows(0) + [r[...] for r in suffix[:1]]
        top[...] = score_pass(query, keys, [0] * 8 + [1], feat, kfeat, scores)

    @pl.when(page_group_ref[1] >= 0)
    def _():
        largest = top[...]
        values = rows(128) + [r[...] for r in suffix[1:]]
        num, total = value_pass(values, scores, largest)
        if own:
            num_ref[...] = num
        else:
            cols = pl.ds(pl.multiple_of(head * HS, HS), HS)
            num_ref[0:TOK, cols] = num.astype(jnp.bfloat16)
        lane = lax.broadcasted_iota(jnp.int32, wide, 1)
        ml[...] = jnp.where(lane == head, largest, jnp.where(lane == head + 8, total, ml[...]))

    @pl.when(head == HEADS_DEV - 1)
    def _():
        rows = ml[...].T[0:16, :]
        if own:
            ml_ref[...] = rows
        else:
            high = rows.astype(jnp.bfloat16)
            rest = rows - high.astype(jnp.float32)
            middle = rest.astype(jnp.bfloat16)
            low = (rest - middle.astype(jnp.float32))[0:8, :]
            low = jnp.concatenate([low[:, 0:HS], low[:, HS:]], axis=0).astype(jnp.bfloat16)
            num_ref[TOK : TOK + 16, :] = jnp.concatenate([high, middle, low], axis=1)


def attend(page_group, query, blocks, suffix=()):
    own = bool(suffix)
    count = 9 if own else 8
    width = HEADS_DEV * HS
    tall = lambda array: pl.BlockSpec((array.shape[0], HS), lambda h, *_: (0, h))
    if own:
        out_shape = (
            jax.ShapeDtypeStruct((TOK, width), jnp.float32),
            jax.ShapeDtypeStruct((16, TOK), jnp.float32),
        )
        out_specs = (
            pl.BlockSpec((TOK, HS), lambda h, *_: (0, h)),
            pl.BlockSpec((16, TOK), lambda h, *_: (0, 0)),
        )
    else:
        out_shape = jax.ShapeDtypeStruct((TOK + 16, width), jnp.bfloat16)
        out_specs = pl.BlockSpec((TOK + 16, width), lambda h, *_: (0, 0))
    operands = (*query, *blocks, *suffix)
    return pl.pallas_call(
        functools.partial(attend_kernel, own, len(query)),
        name="attend_own" if own else "attend",
        out_shape=out_shape,
        grid_spec=pltpu.PrefetchScalarGridSpec(
            num_scalar_prefetch=1,
            grid=(HEADS_DEV,),
            in_specs=[tall(array) for array in operands],
            out_specs=out_specs,
            scratch_shapes=[
                pltpu.VMEM((2, TOK, HS), jnp.bfloat16),
                pltpu.VMEM((9, TOK, HS), jnp.bfloat16),
                pltpu.VMEM((TOK, count * TOK), jnp.float32),
                pltpu.VMEM((TOK, HS), jnp.float32),
                pltpu.VMEM((TOK, HS), jnp.float32),
            ],
        ),
        compiler_params=pltpu.CompilerParams(vmem_limit_bytes=24 << 20),
        cost_estimate=pl.CostEstimate(
            flops=2 * 2 * TOK * TOK * count * HS * HEADS_DEV,
            bytes_accessed=2 * TOK * HS * HEADS_DEV * (2 * count + 3),
            transcendentals=TOK * TOK * count * HEADS_DEV,
        ),
    )(page_group, *operands)


def project_kernel(n0, s0, n1, n2, n3, w_ref, out_ref, att):
    @pl.when(pl.program_id(0) == 0)
    def _():
        tops, sums = [s0[0:8, :]], [s0[8:16, :]]
        for n in (n1, n2, n3):
            piece = n[TOK : TOK + 16, :].astype(jnp.float32)
            low = jnp.concatenate([piece[0:8, 2 * TOK :], piece[8:16, 2 * TOK :]], axis=1)
            tops.append(piece[0:8, :TOK] + piece[0:8, TOK : 2 * TOK] + low)
            sums.append(piece[8:16, :TOK] + piece[8:16, TOK : 2 * TOK])
        best = jnp.maximum(jnp.maximum(tops[0], tops[1]), jnp.maximum(tops[2], tops[3]))
        parts = [jnp.exp2((t - best) * EXP2_SCALE) for t in tops]
        under = sum(p * s for p, s in zip(parts, sums))
        rows = [p / under for p in parts] + [jnp.zeros((96, TOK), jnp.float32)]
        share = jnp.concatenate(rows, axis=0).T
        for h in range(HEADS_DEV):
            cols = slice(h * HS, (h + 1) * HS)
            merged = sum(
                share[:, 8 * i + h : 8 * i + h + 1] * n[0:TOK, cols].astype(jnp.float32)
                for i, n in enumerate((n0, n1, n2, n3))
            )
            att[:, cols] = merged.astype(jnp.bfloat16)

    width = HEADS_DEV * HS
    done = jnp.dot(att[...], w_ref[...], preferred_element_type=jnp.float32)
    out_ref[0] = done[:, :width].astype(jnp.bfloat16)
    out_ref[1] = done[:, width:].astype(jnp.bfloat16)


def project(num, ml, others, weight):
    width = HEADS_DEV * HS
    whole = lambda shape: pl.BlockSpec(shape, lambda j: (0, 0))
    return pl.pallas_call(
        project_kernel,
        name="project",
        out_shape=jax.ShapeDtypeStruct((8, TOK, width), jnp.bfloat16),
        grid=(4,),
        in_specs=[whole((TOK, width)), whole((16, TOK))]
        + [whole((TOK + 16, width))] * 3
        + [pl.BlockSpec((width, 2 * width), lambda j: (0, j))],
        out_specs=pl.BlockSpec((2, TOK, width), lambda j: (j, 0, 0)),
        scratch_shapes=[pltpu.VMEM((TOK, width), jnp.bfloat16)],
        cost_estimate=pl.CostEstimate(
            flops=2 * TOK * width * D,
            bytes_accessed=2 * (width * D + TOK * D) + 3 * 2 * TOK * width,
            transcendentals=TOK * 20,
        ),
    )(num, ml, *others, weight)


def combine_kernel(parts_ref, residual_ref, gate_ref, combined_ref, sums_ref):
    acc = parts_ref[0].astype(jnp.float32)
    for i in range(1, 8):
        acc = acc + parts_ref[i].astype(jnp.float32)
    combined = residual_ref[...].astype(jnp.float32) + gate_ref[...] * acc
    combined_ref[...] = combined
    first = jnp.sum(combined, axis=1, keepdims=True)
    second = jnp.sum(combined * combined, axis=1, keepdims=True)
    lane = lax.broadcasted_iota(jnp.int32, (HS, HS), 1)
    both = jnp.where(lane == 0, first, jnp.where(lane == 1, second, 0.0))
    rows = both.T[0:8, :]
    for i in range(8):
        sums_ref[i] = rows


def combine(parts, residual, gate):
    width = residual.shape[1]
    return pl.pallas_call(
        combine_kernel,
        name="combine",
        grid=(TOK // HS,),
        in_specs=[
            pl.BlockSpec((8, HS, width), lambda i: (0, i, 0)),
            pl.BlockSpec((HS, width), lambda i: (i, 0)),
            pl.BlockSpec((1, width), lambda i: (0, 0)),
        ],
        out_specs=(
            pl.BlockSpec((HS, width), lambda i: (i, 0)),
            pl.BlockSpec((8, 8, HS), lambda i: (0, 0, i)),
        ),
        out_shape=(
            jax.ShapeDtypeStruct((TOK, width), jnp.float32),
            jax.ShapeDtypeStruct((8, 8, TOK), jnp.float32),
        ),
    )(parts, residual, gate)


def finish_kernel(combined_ref, sums_ref, shift_ref, scale_ref, stream_ref, mlp_ref):
    total = sums_ref[0]
    for i in range(1, 8):
        total = total + sums_ref[i]
    mean = total[0:1, :] / D
    variance = total[1:2, :] / D - mean * mean
    inverse = 1.0 / jnp.sqrt(variance + 1e-6)
    rows = lax.broadcasted_iota(jnp.int32, (HS, TOK), 0)
    both = jnp.where(rows == 0, mean, jnp.where(rows == 1, inverse, 0.0)).T
    combined = combined_ref[...]
    stream_ref[...] = combined.astype(jnp.bfloat16)
    normed = (combined - both[:, 0:1]) * both[:, 1:2]
    mlp_ref[...] = (normed * (1.0 + scale_ref[...]) + shift_ref[...]).astype(jnp.bfloat16)


def finish(combined, sums, mod_shift, mod_scale):
    shape = jax.ShapeDtypeStruct(combined.shape, jnp.bfloat16)
    return pl.pallas_call(finish_kernel, name="finish", out_shape=(shape, shape))(
        combined, sums, mod_shift, mod_scale
    )


def body(
    queries,
    suffix_keys,
    suffix_values,
    page_cache,
    page_table,
    suffix_lengths,
    request_group,
    residual,
    out_weight,
    attn_gate,
    mod_shift,
    mod_scale,
):
    width = queries.shape[1]
    send = lambda array, dx, dz, dc: lax.ppermute(array, "req", shift(dx, dz, dc))

    query = pack(suffix_lengths, request_group, queries)
    below = send(query, 0, 1, 0)
    above = send(query, 0, -1, 0)
    opposite = (send(below[:128], 0, 1, 0), send(above[128:], 0, -1, 0))

    pages = page_cache.transpose(0, 2, 1, 3).reshape(2 * TOK, width)
    left, right = send(pages, 1, 0, 0), send(pages, -1, 0, 0)
    over_left = send(left[:TOK], 1, 0, 0)
    over_right = send(right[TOK:], -1, 0, 0)
    across = lambda arrays: arrays + [send(array, 0, 0, 1) for array in arrays]
    blocks = across([pages, left, right]) + across([over_left, over_right])

    me = lax.axis_index("req")
    x, z, c = me // (NZ * NC), (me // NC) % NZ, me % NC
    owners = jnp.stack(
        [rank(x - dx, z, c + dc) for dc in (0, 1) for dx in (0, 1, -1)]
        + [rank(x + 2, z, c), rank(x + 2, z, c + 1)]
    )
    slots = (2 * owners[:, None] + jnp.arange(2, dtype=jnp.int32)[None, :]).reshape(16)
    page_group = jnp.sum((page_table[1][None, :] == slots[:, None]).astype(jnp.int32), 1)

    suffix = (suffix_keys, suffix_values)
    others = []
    for block, dz in ((opposite, 2), ((below,), 1), ((above,), -1)):
        num = attend(page_group, block, blocks)
        others.append(send(num, 0, -dz, 0))
    num, ml = attend(page_group, (query,), blocks, suffix)
    parts = project(num, ml, others, out_weight)
    parts = lax.all_to_all(parts, "tp", 0, 0, tiled=True)
    combined, sums = combine(parts, residual, attn_gate[None, :])
    sums = lax.all_to_all(sums, "tp", 0, 0, tiled=True)
    return finish(combined, sums, mod_shift[None, :], mod_scale[None, :])


def solution(mesh):
    in_specs = (
        P("req", "tp"),
        P("req", "tp"),
        P("req", "tp"),
        P("req", None, None, "tp"),
        P(),
        P("req", None),
        P("req", None),
        P("req", "tp"),
        P("tp", None),
        P("tp"),
        P("tp"),
        P("tp"),
    )
    out_specs = (P("req", "tp"), P("req", "tp"))

    return jax.shard_map(body, mesh=mesh, in_specs=in_specs, out_specs=out_specs, check_vma=False)
```

```python
import functools
import math

import jax
import jax.numpy as jnp
from jax import lax
from jax.experimental import pallas as pl
from jax.experimental.pallas import tpu as pltpu
from jax.sharding import PartitionSpec as P


D = 5120
HS = 128
SPAN = 64
HEADS_DEV = 5
TOK = 256
BIG = -1e30
INV_SQRT = 1.0 / math.sqrt(HS)
EXP2_SCALE = INV_SQRT * math.log2(math.e)


NX, NZ, NC = 4, 4, 2


def rank(x, z, c):
    return ((x % NX) * NZ + z % NZ) * NC + c % NC


def shift(dx, dz, dc):
    return [
        (rank(x, z, c), rank(x + dx, z + dz, c + dc))
        for x in range(NX)
        for z in range(NZ)
        for c in range(NC)
    ]


def token_facts(facts, shape):
    lane = lax.broadcasted_iota(jnp.int32, facts.shape, 1)
    pick = lambda j: jnp.sum(jnp.where(lane == j, facts, 0.0), axis=1, keepdims=True)
    lens = [pick(j).astype(jnp.int32) for j in range(3)]
    groups = [pick(4 + j).astype(jnp.int32) for j in range(4)]
    pos = lax.broadcasted_iota(jnp.int32, shape, 0)
    e0 = lens[0]
    e1 = e0 + lens[1]
    e2 = e1 + lens[2]
    after0, after1, after2 = pos >= e0, pos >= e1, pos >= e2
    request = jnp.where(after2, 3, jnp.where(after1, 2, jnp.where(after0, 1, 0)))
    start = jnp.where(after2, e2, jnp.where(after1, e1, jnp.where(after0, e0, 0)))
    group = jnp.where(
        after2, groups[3], jnp.where(after1, groups[2], jnp.where(after0, groups[1], groups[0]))
    )
    block = jnp.where(pos - start >= SPAN, 1, 0)
    return request, block, group


def pack_kernel(lens_ref, groups_ref, q_ref, out_ref):
    width = q_ref.shape[1]
    out_ref[0:TOK, :] = q_ref[...]
    lane = lax.broadcasted_iota(jnp.int32, (16, width), 1)
    facts = jnp.zeros((16, width), jnp.int32)
    for i in range(4):
        facts = jnp.where(lane == i, lens_ref[0, i], facts)
        facts = jnp.where(lane == 4 + i, groups_ref[0, i], facts)
    out_ref[TOK : TOK + 16, :] = facts.astype(jnp.float32).astype(jnp.bfloat16)


def pack(lens, groups, queries):
    smem = pl.BlockSpec(memory_space=pltpu.SMEM)
    return pl.pallas_call(
        pack_kernel,
        name="pack",
        in_specs=[smem, smem, pl.BlockSpec(memory_space=pltpu.VMEM)],
        out_specs=pl.BlockSpec(memory_space=pltpu.VMEM),
        out_shape=jax.ShapeDtypeStruct((TOK + 16, queries.shape[1]), queries.dtype),
    )(lens, groups, queries)


def features(own, facts, page_group_ref, feat, kfeat):
    wide = (TOK, HS)
    request, block, group = token_facts(facts.astype(jnp.float32)[0:1, :], wide)
    lane = lax.broadcasted_iota(jnp.int32, wide, 1)
    row = lax.broadcasted_iota(jnp.int32, wide, 0)
    feat[0] = jnp.where(lane == group, 1.0, 0.0).astype(jnp.bfloat16)
    for i in range(8):
        low, high = page_group_ref[2 * i], page_group_ref[2 * i + 1]
        hidden = (lane < 2) & (lane != jnp.where(row < 128, low, high))
        kfeat[i] = jnp.where(hidden, BIG, 0.0).astype(jnp.bfloat16)
    if own:
        feat[1] = jnp.where(lane == 2 * request + block, 1.0, 0.0).astype(jnp.bfloat16)
        seen = (request == lane // 2) & (block <= lane % 2)
        kfeat[8] = jnp.where((lane < 8) & ~seen, BIG, 0.0).astype(jnp.bfloat16)


def score_pass(query, keys, marks, feat, kfeat, scores):
    best = None
    for i, (key, mark) in enumerate(zip(keys, marks)):
        left = jnp.concatenate([query, feat[mark]], axis=1)
        right = jnp.concatenate([key, kfeat[i]], axis=1)
        score = lax.dot_general(
            left, right, (((1,), (1,)), ((), ())), preferred_element_type=jnp.float32
        )
        scores[:, i * TOK : (i + 1) * TOK] = score
        here = jnp.maximum(score[:, :HS], score[:, HS:])
        best = here if best is None else jnp.maximum(best, here)
    return jnp.broadcast_to(jnp.max(best, axis=1, keepdims=True), (TOK, HS))


def value_pass(values, scores, largest):
    both = jnp.concatenate([largest, largest], axis=1)
    ones = jnp.ones((TOK, HS), jnp.bfloat16)
    total = None
    for i, value in enumerate(values):
        weight = jnp.exp2((scores[:, i * TOK : (i + 1) * TOK] - both) * EXP2_SCALE)
        part = jnp.dot(
            weight.astype(jnp.bfloat16),
            jnp.concatenate([value, ones], axis=1),
            preferred_element_type=jnp.float32,
        )
        total = part if total is None else total + part
    return total[:, :HS], total[:, HS:]


def attend_kernel(own, pieces, page_group_ref, *refs):
    q_refs, refs = refs[:pieces], refs[pieces:]
    kv_refs, refs = refs[:10], refs[10:]
    suffix, refs = (refs[:2], refs[2:]) if own else ((), refs)
    if own:
        num_ref, ml_ref, feat, kfeat, scores, top, ml = refs
    else:
        num_ref, feat, kfeat, scores, top, ml = refs
    head = pl.program_id(0)
    wide = (TOK, HS)

    @pl.when(head == 0)
    def _():
        facts = q_refs[-1][TOK // pieces : TOK // pieces + 16, :]
        features(own, facts, page_group_ref, feat, kfeat)
        ml[...] = jnp.zeros_like(ml)

    def rows(start):
        pick = slice(start, start + 128)
        later = slice(start + 256, start + 384)
        out = [jnp.concatenate([r[pick, :], r[later, :]], axis=0) for r in kv_refs[:6]]
        for a, b in (kv_refs[6:8], kv_refs[8:10]):
            out.append(jnp.concatenate([a[pick, :], b[pick, :]], axis=0))
        return out

    @pl.when(page_group_ref[0] >= 0)
    def _():
        if pieces == 1:
            query = q_refs[0][0:TOK, :]
        else:
            query = jnp.concatenate([q_refs[0][...], q_refs[1][0:128, :]], axis=0)
        keys = rows(0) + [r[...] for r in suffix[:1]]
        top[...] = score_pass(query, keys, [0] * 8 + [1], feat, kfeat, scores)

    @pl.when(page_group_ref[1] >= 0)
    def _():
        largest = top[...]
        values = rows(128) + [r[...] for r in suffix[1:]]
        num, total = value_pass(values, scores, largest)
        if own:
            num_ref[...] = num
        else:
            cols = pl.ds(pl.multiple_of(head * HS, HS), HS)
            num_ref[0:TOK, cols] = num.astype(jnp.bfloat16)
        lane = lax.broadcasted_iota(jnp.int32, wide, 1)
        ml[...] = jnp.where(lane == head, largest, jnp.where(lane == head + 8, total, ml[...]))

    @pl.when(head == HEADS_DEV - 1)
    def _():
        rows = ml[...].T[0:16, :]
        if own:
            ml_ref[...] = rows
        else:
            high = rows.astype(jnp.bfloat16)
            rest = rows - high.astype(jnp.float32)
            middle = rest.astype(jnp.bfloat16)
            low = (rest - middle.astype(jnp.float32))[0:8, :]
            low = jnp.concatenate([low[:, 0:HS], low[:, HS:]], axis=0).astype(jnp.bfloat16)
            num_ref[TOK : TOK + 16, :] = jnp.concatenate([high, middle, low], axis=1)


def attend(page_group, query, blocks, suffix=()):
    own = bool(suffix)
    count = 9 if own else 8
    width = HEADS_DEV * HS
    tall = lambda array: pl.BlockSpec((array.shape[0], HS), lambda h, *_: (0, h))
    if own:
        out_shape = (
            jax.ShapeDtypeStruct((TOK, width), jnp.float32),
            jax.ShapeDtypeStruct((16, TOK), jnp.float32),
        )
        out_specs = (
            pl.BlockSpec((TOK, HS), lambda h, *_: (0, h)),
            pl.BlockSpec((16, TOK), lambda h, *_: (0, 0)),
        )
    else:
        out_shape = jax.ShapeDtypeStruct((TOK + 16, width), jnp.bfloat16)
        out_specs = pl.BlockSpec((TOK + 16, width), lambda h, *_: (0, 0))
    operands = (*query, *blocks, *suffix)
    return pl.pallas_call(
        functools.partial(attend_kernel, own, len(query)),
        name="attend_own" if own else "attend",
        out_shape=out_shape,
        grid_spec=pltpu.PrefetchScalarGridSpec(
            num_scalar_prefetch=1,
            grid=(HEADS_DEV,),
            in_specs=[tall(array) for array in operands],
            out_specs=out_specs,
            scratch_shapes=[
                pltpu.VMEM((2, TOK, HS), jnp.bfloat16),
                pltpu.VMEM((9, TOK, HS), jnp.bfloat16),
                pltpu.VMEM((TOK, count * TOK), jnp.float32),
                pltpu.VMEM((TOK, HS), jnp.float32),
                pltpu.VMEM((TOK, HS), jnp.float32),
            ],
        ),
        compiler_params=pltpu.CompilerParams(vmem_limit_bytes=24 << 20),
        cost_estimate=pl.CostEstimate(
            flops=2 * 2 * TOK * TOK * count * HS * HEADS_DEV,
            bytes_accessed=2 * TOK * HS * HEADS_DEV * (2 * count + 3),
            transcendentals=TOK * TOK * count * HEADS_DEV,
        ),
    )(page_group, *operands)


def project_kernel(n0, s0, n1, n2, n3, w_ref, out_ref, att):
    @pl.when(pl.program_id(0) == 0)
    def _():
        tops, sums = [s0[0:8, :]], [s0[8:16, :]]
        for n in (n1, n2, n3):
            piece = n[TOK : TOK + 16, :].astype(jnp.float32)
            low = jnp.concatenate([piece[0:8, 2 * TOK :], piece[8:16, 2 * TOK :]], axis=1)
            tops.append(piece[0:8, :TOK] + piece[0:8, TOK : 2 * TOK] + low)
            sums.append(piece[8:16, :TOK] + piece[8:16, TOK : 2 * TOK])
        best = jnp.maximum(jnp.maximum(tops[0], tops[1]), jnp.maximum(tops[2], tops[3]))
        parts = [jnp.exp2((t - best) * EXP2_SCALE) for t in tops]
        under = sum(p * s for p, s in zip(parts, sums))
        rows = [p / under for p in parts] + [jnp.zeros((96, TOK), jnp.float32)]
        share = jnp.concatenate(rows, axis=0).T
        for h in range(HEADS_DEV):
            cols = slice(h * HS, (h + 1) * HS)
            merged = sum(
                share[:, 8 * i + h : 8 * i + h + 1] * n[0:TOK, cols].astype(jnp.float32)
                for i, n in enumerate((n0, n1, n2, n3))
            )
            att[:, cols] = merged.astype(jnp.bfloat16)

    width = HEADS_DEV * HS
    done = jnp.dot(att[...], w_ref[...], preferred_element_type=jnp.float32)
    out_ref[0] = done[:, :width].astype(jnp.bfloat16)
    out_ref[1] = done[:, width:].astype(jnp.bfloat16)


def project(num, ml, others, weight):
    width = HEADS_DEV * HS
    whole = lambda shape: pl.BlockSpec(shape, lambda j: (0, 0))
    return pl.pallas_call(
        project_kernel,
        name="project",
        out_shape=pltpu.HBM((8, TOK, width), jnp.bfloat16),
        grid=(4,),
        in_specs=[whole((TOK, width)), whole((16, TOK))]
        + [whole((TOK + 16, width))] * 3
        + [pl.BlockSpec((width, 2 * width), lambda j: (0, j))],
        out_specs=pl.BlockSpec((2, TOK, width), lambda j: (j, 0, 0)),
        scratch_shapes=[pltpu.VMEM((TOK, width), jnp.bfloat16)],
        compiler_params=pltpu.CompilerParams(vmem_limit_bytes=24 << 20),
        cost_estimate=pl.CostEstimate(
            flops=2 * TOK * width * D,
            bytes_accessed=2 * (width * D + TOK * D) + 3 * 2 * TOK * width,
            transcendentals=TOK * 20,
        ),
    )(num, ml, *others, weight)


def combine_kernel(parts_ref, residual_ref, gate_ref, combined_ref, sums_ref):
    acc = parts_ref[0].astype(jnp.float32)
    for i in range(1, 8):
        acc = acc + parts_ref[i].astype(jnp.float32)
    combined = residual_ref[...].astype(jnp.float32) + gate_ref[...] * acc
    combined_ref[...] = combined
    first = jnp.sum(combined, axis=1, keepdims=True)
    second = jnp.sum(combined * combined, axis=1, keepdims=True)
    lane = lax.broadcasted_iota(jnp.int32, (HS, HS), 1)
    both = jnp.where(lane == 0, first, jnp.where(lane == 1, second, 0.0))
    rows = both.T[0:8, :]
    for i in range(8):
        sums_ref[i] = rows


def combine(parts, residual, gate):
    width = residual.shape[1]
    return pl.pallas_call(
        combine_kernel,
        name="combine",
        grid=(TOK // HS,),
        in_specs=[
            pl.BlockSpec((8, HS, width), lambda i: (0, i, 0)),
            pl.BlockSpec((HS, width), lambda i: (i, 0)),
            pl.BlockSpec((1, width), lambda i: (0, 0)),
        ],
        out_specs=(
            pl.BlockSpec((HS, width), lambda i: (i, 0)),
            pl.BlockSpec((8, 8, HS), lambda i: (0, 0, i)),
        ),
        out_shape=(
            jax.ShapeDtypeStruct((TOK, width), jnp.float32),
            jax.ShapeDtypeStruct((8, 8, TOK), jnp.float32),
        ),
        compiler_params=pltpu.CompilerParams(vmem_limit_bytes=16 << 20),
    )(parts, residual, gate)


def finish_kernel(combined_ref, sums_ref, shift_ref, scale_ref, stream_ref, mlp_ref):
    total = sums_ref[0]
    for i in range(1, 8):
        total = total + sums_ref[i]
    mean = total[0:1, :] / D
    variance = total[1:2, :] / D - mean * mean
    inverse = 1.0 / jnp.sqrt(variance + 1e-6)
    rows = lax.broadcasted_iota(jnp.int32, (HS, TOK), 0)
    both = jnp.where(rows == 0, mean, jnp.where(rows == 1, inverse, 0.0)).T
    combined = combined_ref[...]
    stream_ref[...] = combined.astype(jnp.bfloat16)
    normed = (combined - both[:, 0:1]) * both[:, 1:2]
    mlp_ref[...] = (normed * (1.0 + scale_ref[...]) + shift_ref[...]).astype(jnp.bfloat16)


def finish(combined, sums, mod_shift, mod_scale):
    shape = jax.ShapeDtypeStruct(combined.shape, jnp.bfloat16)
    return pl.pallas_call(
        finish_kernel,
        name="finish",
        out_shape=(shape, shape),
        compiler_params=pltpu.CompilerParams(vmem_limit_bytes=16 << 20),
    )(combined, sums, mod_shift, mod_scale)


def body(
    queries,
    suffix_keys,
    suffix_values,
    page_cache,
    page_table,
    suffix_lengths,
    request_group,
    residual,
    out_weight,
    attn_gate,
    mod_shift,
    mod_scale,
):
    width = queries.shape[1]
    send = lambda array, dx, dz, dc: lax.ppermute(array, "req", shift(dx, dz, dc))

    query = pack(suffix_lengths, request_group, queries)
    below = send(query, 0, 1, 0)
    above = send(query, 0, -1, 0)
    opposite = send(query, 0, 2, 0)

    pages = page_cache.transpose(0, 2, 1, 3).reshape(2 * TOK, width)
    left, right = send(pages, 1, 0, 0), send(pages, -1, 0, 0)
    over_left = send(left[:TOK], 1, 0, 0)
    over_right = send(right[TOK:], -1, 0, 0)
    across = lambda arrays: arrays + [send(array, 0, 0, 1) for array in arrays]
    blocks = across([pages, left, right]) + across([over_left, over_right])

    me = lax.axis_index("req")
    x, z, c = me // (NZ * NC), (me // NC) % NZ, me % NC
    owners = jnp.stack(
        [rank(x - dx, z, c + dc) for dc in (0, 1) for dx in (0, 1, -1)]
        + [rank(x + 2, z, c), rank(x + 2, z, c + 1)]
    )
    slots = (2 * owners[:, None] + jnp.arange(2, dtype=jnp.int32)[None, :]).reshape(16)
    page_group = jnp.sum((page_table[1][None, :] == slots[:, None]).astype(jnp.int32), 1)

    suffix = (suffix_keys, suffix_values)
    others = []
    for block, dz in ((below, 1), (opposite, 2), (above, -1)):
        num = attend(page_group, (block,), blocks)
        others.append(send(num, 0, -dz, 0))
    num, ml = attend(page_group, (query,), blocks, suffix)
    parts = project(num, ml, others, out_weight)
    parts = lax.all_to_all(parts, "tp", 0, 0, tiled=True)
    combined, sums = combine(parts, residual, attn_gate[None, :])
    sums = lax.all_to_all(sums, "tp", 0, 0, tiled=True)
    return finish(combined, sums, mod_shift[None, :], mod_scale[None, :])


def solution(mesh):
    in_specs = (
        P("req", "tp"),
        P("req", "tp"),
        P("req", "tp"),
        P("req", None, None, "tp"),
        P(),
        P("req", None),
        P("req", None),
        P("req", "tp"),
        P("tp", None),
        P("tp"),
        P("tp"),
        P("tp"),
    )
    out_specs = (P("req", "tp"), P("req", "tp"))

    return jax.shard_map(body, mesh=mesh, in_specs=in_specs, out_specs=out_specs, check_vma=False)
```

```python
import functools
import math

import jax
import jax.numpy as jnp
from jax import lax
from jax.experimental import pallas as pl
from jax.experimental.pallas import tpu as pltpu
from jax.sharding import PartitionSpec as P


D = 5120
HS = 128
SPAN = 64
HEADS_DEV = 5
TOK = 256
BIG = -1e30
INV_SQRT = 1.0 / math.sqrt(HS)
EXP2_SCALE = INV_SQRT * math.log2(math.e)


NX, NZ, NC = 4, 4, 2


def rank(x, z, c):
    return ((x % NX) * NZ + z % NZ) * NC + c % NC


def shift(dx, dz, dc):
    return [
        (rank(x, z, c), rank(x + dx, z + dz, c + dc))
        for x in range(NX)
        for z in range(NZ)
        for c in range(NC)
    ]


def token_facts(facts, shape):
    lane = lax.broadcasted_iota(jnp.int32, facts.shape, 1)
    pick = lambda j: jnp.sum(jnp.where(lane == j, facts, 0.0), axis=1, keepdims=True)
    lens = [pick(j).astype(jnp.int32) for j in range(3)]
    groups = [pick(4 + j).astype(jnp.int32) for j in range(4)]
    pos = lax.broadcasted_iota(jnp.int32, shape, 0)
    e0 = lens[0]
    e1 = e0 + lens[1]
    e2 = e1 + lens[2]
    after0, after1, after2 = pos >= e0, pos >= e1, pos >= e2
    request = jnp.where(after2, 3, jnp.where(after1, 2, jnp.where(after0, 1, 0)))
    start = jnp.where(after2, e2, jnp.where(after1, e1, jnp.where(after0, e0, 0)))
    group = jnp.where(
        after2, groups[3], jnp.where(after1, groups[2], jnp.where(after0, groups[1], groups[0]))
    )
    block = jnp.where(pos - start >= SPAN, 1, 0)
    return request, block, group


def features(own, facts, page_group_ref, feat, kfeat):
    wide = (TOK, HS)
    request, block, group = token_facts(facts, wide)
    lane = lax.broadcasted_iota(jnp.int32, wide, 1)
    row = lax.broadcasted_iota(jnp.int32, wide, 0)
    feat[0] = jnp.where(lane == group, 1.0, 0.0).astype(jnp.bfloat16)
    for i in range(8):
        low, high = page_group_ref[2 * i], page_group_ref[2 * i + 1]
        hidden = (lane < 2) & (lane != jnp.where(row < 128, low, high))
        kfeat[i] = jnp.where(hidden, BIG, 0.0).astype(jnp.bfloat16)
    if own:
        feat[1] = jnp.where(lane == 2 * request + block, 1.0, 0.0).astype(jnp.bfloat16)
        seen = (request == lane // 2) & (block <= lane % 2)
        kfeat[8] = jnp.where((lane < 8) & ~seen, BIG, 0.0).astype(jnp.bfloat16)


def score_pass(query, keys, marks, feat, kfeat, scores):
    best = None
    for i, (key, mark) in enumerate(zip(keys, marks)):
        left = jnp.concatenate([query, feat[mark]], axis=1)
        right = jnp.concatenate([key, kfeat[i]], axis=1)
        score = lax.dot_general(
            left, right, (((1,), (1,)), ((), ())), preferred_element_type=jnp.float32
        )
        scores[:, i * TOK : (i + 1) * TOK] = score
        here = jnp.maximum(score[:, :HS], score[:, HS:])
        best = here if best is None else jnp.maximum(best, here)
    return jnp.broadcast_to(jnp.max(best, axis=1, keepdims=True), (TOK, HS))


def value_pass(values, scores, largest):
    both = jnp.concatenate([largest, largest], axis=1)
    ones = jnp.ones((TOK, HS), jnp.bfloat16)
    total = None
    for i, value in enumerate(values):
        weight = jnp.exp2((scores[:, i * TOK : (i + 1) * TOK] - both) * EXP2_SCALE)
        part = jnp.dot(
            weight.astype(jnp.bfloat16),
            jnp.concatenate([value, ones], axis=1),
            preferred_element_type=jnp.float32,
        )
        total = part if total is None else total + part
    return total[:, :HS], total[:, HS:]


def attend_kernel(own, page_group_ref, facts_ref, q_ref, *refs):
    kv_refs, refs = refs[:10], refs[10:]
    suffix, refs = (refs[:2], refs[2:]) if own else ((), refs)
    if own:
        num_ref, ml_ref, feat, kfeat, scores, top, ml = refs
    else:
        num_ref, feat, kfeat, scores, top, ml = refs
    head = pl.program_id(0)
    wide = (TOK, HS)

    @pl.when(head == 0)
    def _():
        features(own, facts_ref[...].astype(jnp.float32), page_group_ref, feat, kfeat)
        ml[...] = jnp.zeros_like(ml)

    def rows(start):
        pick = slice(start, start + 128)
        later = slice(start + 256, start + 384)
        out = [jnp.concatenate([r[pick, :], r[later, :]], axis=0) for r in kv_refs[:6]]
        for a, b in (kv_refs[6:8], kv_refs[8:10]):
            out.append(jnp.concatenate([a[pick, :], b[pick, :]], axis=0))
        return out

    @pl.when(page_group_ref[0] >= 0)
    def _():
        query = q_ref[...]
        keys = rows(0) + [r[...] for r in suffix[:1]]
        top[...] = score_pass(query, keys, [0] * 8 + [1], feat, kfeat, scores)

    @pl.when(page_group_ref[1] >= 0)
    def _():
        largest = top[...]
        values = rows(128) + [r[...] for r in suffix[1:]]
        num, total = value_pass(values, scores, largest)
        if own:
            num_ref[...] = num
        else:
            cols = pl.ds(pl.multiple_of(head * HS, HS), HS)
            num_ref[0:TOK, cols] = num.astype(jnp.bfloat16)
        lane = lax.broadcasted_iota(jnp.int32, wide, 1)
        ml[...] = jnp.where(lane == head, largest, jnp.where(lane == head + 8, total, ml[...]))

    @pl.when(head == HEADS_DEV - 1)
    def _():
        rows = ml[...].T[0:16, :]
        if own:
            ml_ref[...] = rows
        else:
            high = rows.astype(jnp.bfloat16)
            rest = rows - high.astype(jnp.float32)
            middle = rest.astype(jnp.bfloat16)
            low = (rest - middle.astype(jnp.float32))[0:8, :]
            low = jnp.concatenate([low[:, 0:HS], low[:, HS:]], axis=0).astype(jnp.bfloat16)
            num_ref[TOK : TOK + 16, :] = jnp.concatenate([high, middle, low], axis=1)


def attend(page_group, facts, query, blocks, suffix=()):
    own = bool(suffix)
    count = 9 if own else 8
    width = HEADS_DEV * HS
    tall = lambda array: pl.BlockSpec((array.shape[0], HS), lambda h, *_: (0, h))
    if own:
        out_shape = (
            jax.ShapeDtypeStruct((TOK, width), jnp.float32),
            jax.ShapeDtypeStruct((16, TOK), jnp.float32),
        )
        out_specs = (
            pl.BlockSpec((TOK, HS), lambda h, *_: (0, h)),
            pl.BlockSpec((16, TOK), lambda h, *_: (0, 0)),
        )
    else:
        out_shape = jax.ShapeDtypeStruct((TOK + 16, width), jnp.bfloat16)
        out_specs = pl.BlockSpec((TOK + 16, width), lambda h, *_: (0, 0))
    operands = (query, *blocks, *suffix)
    return pl.pallas_call(
        functools.partial(attend_kernel, own),
        name="attend_own" if own else "attend",
        out_shape=out_shape,
        grid_spec=pltpu.PrefetchScalarGridSpec(
            num_scalar_prefetch=1,
            grid=(HEADS_DEV,),
            in_specs=[pl.BlockSpec((1, 8), lambda h, *_: (0, 0))]
            + [tall(array) for array in operands],
            out_specs=out_specs,
            scratch_shapes=[
                pltpu.VMEM((2, TOK, HS), jnp.bfloat16),
                pltpu.VMEM((9, TOK, HS), jnp.bfloat16),
                pltpu.VMEM((TOK, count * TOK), jnp.float32),
                pltpu.VMEM((TOK, HS), jnp.float32),
                pltpu.VMEM((TOK, HS), jnp.float32),
            ],
        ),
        compiler_params=pltpu.CompilerParams(vmem_limit_bytes=24 << 20),
        cost_estimate=pl.CostEstimate(
            flops=2 * 2 * TOK * TOK * count * HS * HEADS_DEV,
            bytes_accessed=2 * TOK * HS * HEADS_DEV * (2 * count + 3),
            transcendentals=TOK * TOK * count * HEADS_DEV,
        ),
    )(page_group, facts, *operands)


def project_kernel(n0, s0, n1, n2, n3, w_ref, out_ref, att):
    @pl.when(pl.program_id(0) == 0)
    def _():
        tops, sums = [s0[0:8, :]], [s0[8:16, :]]
        for n in (n1, n2, n3):
            piece = n[TOK : TOK + 16, :].astype(jnp.float32)
            low = jnp.concatenate([piece[0:8, 2 * TOK :], piece[8:16, 2 * TOK :]], axis=1)
            tops.append(piece[0:8, :TOK] + piece[0:8, TOK : 2 * TOK] + low)
            sums.append(piece[8:16, :TOK] + piece[8:16, TOK : 2 * TOK])
        best = jnp.maximum(jnp.maximum(tops[0], tops[1]), jnp.maximum(tops[2], tops[3]))
        parts = [jnp.exp2((t - best) * EXP2_SCALE) for t in tops]
        under = sum(p * s for p, s in zip(parts, sums))
        rows = [p / under for p in parts] + [jnp.zeros((96, TOK), jnp.float32)]
        share = jnp.concatenate(rows, axis=0).T
        for h in range(HEADS_DEV):
            cols = slice(h * HS, (h + 1) * HS)
            merged = sum(
                share[:, 8 * i + h : 8 * i + h + 1] * n[0:TOK, cols].astype(jnp.float32)
                for i, n in enumerate((n0, n1, n2, n3))
            )
            att[:, cols] = merged.astype(jnp.bfloat16)

    width = HEADS_DEV * HS
    done = jnp.dot(att[...], w_ref[...], preferred_element_type=jnp.float32)
    out_ref[0] = done[:, :width].astype(jnp.bfloat16)
    out_ref[1] = done[:, width:].astype(jnp.bfloat16)


def project(num, ml, others, weight):
    width = HEADS_DEV * HS
    whole = lambda shape: pl.BlockSpec(shape, lambda j: (0, 0))
    return pl.pallas_call(
        project_kernel,
        name="project",
        out_shape=pltpu.HBM((8, TOK, width), jnp.bfloat16),
        grid=(4,),
        in_specs=[whole((TOK, width)), whole((16, TOK))]
        + [whole((TOK + 16, width))] * 3
        + [pl.BlockSpec((width, 2 * width), lambda j: (0, j))],
        out_specs=pl.BlockSpec((2, TOK, width), lambda j: (j, 0, 0)),
        scratch_shapes=[pltpu.VMEM((TOK, width), jnp.bfloat16)],
        compiler_params=pltpu.CompilerParams(vmem_limit_bytes=24 << 20),
        cost_estimate=pl.CostEstimate(
            flops=2 * TOK * width * D,
            bytes_accessed=2 * (width * D + TOK * D) + 3 * 2 * TOK * width,
            transcendentals=TOK * 20,
        ),
    )(num, ml, *others, weight)


def combine_kernel(parts_ref, residual_ref, gate_ref, combined_ref, sums_ref):
    acc = parts_ref[0].astype(jnp.float32)
    for i in range(1, 8):
        acc = acc + parts_ref[i].astype(jnp.float32)
    combined = residual_ref[...].astype(jnp.float32) + gate_ref[...] * acc
    combined_ref[...] = combined
    first = jnp.sum(combined, axis=1, keepdims=True)
    second = jnp.sum(combined * combined, axis=1, keepdims=True)
    lane = lax.broadcasted_iota(jnp.int32, (HS, HS), 1)
    both = jnp.where(lane == 0, first, jnp.where(lane == 1, second, 0.0))
    rows = both.T[0:8, :]
    for i in range(8):
        sums_ref[i] = rows


def combine(parts, residual, gate):
    width = residual.shape[1]
    return pl.pallas_call(
        combine_kernel,
        name="combine",
        grid=(TOK // HS,),
        in_specs=[
            pl.BlockSpec((8, HS, width), lambda i: (0, i, 0)),
            pl.BlockSpec((HS, width), lambda i: (i, 0)),
            pl.BlockSpec((1, width), lambda i: (0, 0)),
        ],
        out_specs=(
            pl.BlockSpec((HS, width), lambda i: (i, 0)),
            pl.BlockSpec((8, 8, HS), lambda i: (0, 0, i)),
        ),
        out_shape=(
            jax.ShapeDtypeStruct((TOK, width), jnp.float32),
            jax.ShapeDtypeStruct((8, 8, TOK), jnp.float32),
        ),
        compiler_params=pltpu.CompilerParams(vmem_limit_bytes=16 << 20),
    )(parts, residual, gate)


def finish_kernel(combined_ref, sums_ref, shift_ref, scale_ref, stream_ref, mlp_ref):
    total = sums_ref[0]
    for i in range(1, 8):
        total = total + sums_ref[i]
    mean = total[0:1, :] / D
    variance = total[1:2, :] / D - mean * mean
    inverse = 1.0 / jnp.sqrt(variance + 1e-6)
    rows = lax.broadcasted_iota(jnp.int32, (HS, TOK), 0)
    both = jnp.where(rows == 0, mean, jnp.where(rows == 1, inverse, 0.0)).T
    combined = combined_ref[...]
    stream_ref[...] = combined.astype(jnp.bfloat16)
    normed = (combined - both[:, 0:1]) * both[:, 1:2]
    mlp_ref[...] = (normed * (1.0 + scale_ref[...]) + shift_ref[...]).astype(jnp.bfloat16)


def finish(combined, sums, mod_shift, mod_scale):
    shape = jax.ShapeDtypeStruct(combined.shape, jnp.bfloat16)
    return pl.pallas_call(
        finish_kernel,
        name="finish",
        out_shape=(shape, shape),
        compiler_params=pltpu.CompilerParams(vmem_limit_bytes=16 << 20),
    )(combined, sums, mod_shift, mod_scale)


def body(
    queries,
    suffix_keys,
    suffix_values,
    page_cache,
    page_table,
    suffix_lengths,
    request_group,
    residual,
    out_weight,
    attn_gate,
    mod_shift,
    mod_scale,
):
    width = queries.shape[1]
    send = lambda array, dx, dz, dc: lax.ppermute(array, "req", shift(dx, dz, dc))

    ways = (1, -1, 2)
    facts = jnp.concatenate([suffix_lengths, request_group], axis=1)
    their_query = [send(queries, 0, dz, 0) for dz in ways]
    their_facts = [send(facts, 0, dz, 0) for dz in ways]

    pages = page_cache.transpose(0, 2, 1, 3).reshape(2 * TOK, width)
    left, right = send(pages, 1, 0, 0), send(pages, -1, 0, 0)
    over_left = send(left[:TOK], 1, 0, 0)
    over_right = send(right[TOK:], -1, 0, 0)
    across = lambda arrays: arrays + [send(array, 0, 0, 1) for array in arrays]
    blocks = across([pages, left, right]) + across([over_left, over_right])

    me = lax.axis_index("req")
    x, z, c = me // (NZ * NC), (me // NC) % NZ, me % NC
    owners = jnp.stack(
        [rank(x - dx, z, c + dc) for dc in (0, 1) for dx in (0, 1, -1)]
        + [rank(x + 2, z, c), rank(x + 2, z, c + 1)]
    )
    slots = (2 * owners[:, None] + jnp.arange(2, dtype=jnp.int32)[None, :]).reshape(16)
    page_group = jnp.sum((page_table[1][None, :] == slots[:, None]).astype(jnp.int32), 1)

    suffix = (suffix_keys, suffix_values)
    others = []
    for i, dz in enumerate(ways):
        num = attend(page_group, their_facts[i], their_query[i], blocks)
        others.append(send(num, 0, -dz, 0))
    num, ml = attend(page_group, facts, queries, blocks, suffix)
    parts = project(num, ml, others, out_weight)
    parts = lax.all_to_all(parts, "tp", 0, 0, tiled=True)
    combined, sums = combine(parts, residual, attn_gate[None, :])
    sums = lax.all_to_all(sums, "tp", 0, 0, tiled=True)
    return finish(combined, sums, mod_shift[None, :], mod_scale[None, :])


def solution(mesh):
    in_specs = (
        P("req", "tp"),
        P("req", "tp"),
        P("req", "tp"),
        P("req", None, None, "tp"),
        P(),
        P("req", None),
        P("req", None),
        P("req", "tp"),
        P("tp", None),
        P("tp"),
        P("tp"),
        P("tp"),
    )
    out_specs = (P("req", "tp"), P("req", "tp"))

    return jax.shard_map(body, mesh=mesh, in_specs=in_specs, out_specs=out_specs, check_vma=False)
```

```python
import functools
import math

import jax
import jax.numpy as jnp
from jax import lax
from jax.experimental import pallas as pl
from jax.experimental.pallas import tpu as pltpu
from jax.sharding import PartitionSpec as P


D = 5120
HS = 128
SPAN = 64
HEADS_DEV = 5
TOK = 256
BIG = -1e30
INV_SQRT = 1.0 / math.sqrt(HS)
EXP2_SCALE = INV_SQRT * math.log2(math.e)


NX, NZ, NC = 4, 4, 2


def rank(x, z, c):
    return ((x % NX) * NZ + z % NZ) * NC + c % NC


def shift(dx, dz, dc):
    return [
        (rank(x, z, c), rank(x + dx, z + dz, c + dc))
        for x in range(NX)
        for z in range(NZ)
        for c in range(NC)
    ]


def token_facts(facts, shape):
    lane = lax.broadcasted_iota(jnp.int32, facts.shape, 1)
    pick = lambda j: jnp.sum(jnp.where(lane == j, facts, 0.0), axis=1, keepdims=True)
    lens = [pick(j).astype(jnp.int32) for j in range(3)]
    groups = [pick(4 + j).astype(jnp.int32) for j in range(4)]
    pos = lax.broadcasted_iota(jnp.int32, shape, 0)
    e0 = lens[0]
    e1 = e0 + lens[1]
    e2 = e1 + lens[2]
    after0, after1, after2 = pos >= e0, pos >= e1, pos >= e2
    request = jnp.where(after2, 3, jnp.where(after1, 2, jnp.where(after0, 1, 0)))
    start = jnp.where(after2, e2, jnp.where(after1, e1, jnp.where(after0, e0, 0)))
    group = jnp.where(
        after2, groups[3], jnp.where(after1, groups[2], jnp.where(after0, groups[1], groups[0]))
    )
    block = jnp.where(pos - start >= SPAN, 1, 0)
    return request, block, group


def features(own, facts, page_group_ref, feat, kfeat):
    wide = (TOK, HS)
    request, block, group = token_facts(facts, wide)
    lane = lax.broadcasted_iota(jnp.int32, wide, 1)
    row = lax.broadcasted_iota(jnp.int32, wide, 0)
    feat[0] = jnp.where(lane == group, 1.0, 0.0).astype(jnp.bfloat16)
    for i in range(8):
        low, high = page_group_ref[2 * i], page_group_ref[2 * i + 1]
        hidden = (lane < 2) & (lane != jnp.where(row < 128, low, high))
        kfeat[i] = jnp.where(hidden, BIG, 0.0).astype(jnp.bfloat16)
    if own:
        feat[1] = jnp.where(lane == 2 * request + block, 1.0, 0.0).astype(jnp.bfloat16)
        seen = (request == lane // 2) & (block <= lane % 2)
        kfeat[8] = jnp.where((lane < 8) & ~seen, BIG, 0.0).astype(jnp.bfloat16)


def score_pass(query, keys, marks, feat, kfeat, scores):
    best = None
    for i, (key, mark) in enumerate(zip(keys, marks)):
        left = jnp.concatenate([query, feat[mark]], axis=1)
        right = jnp.concatenate([key, kfeat[i]], axis=1)
        score = lax.dot_general(
            left, right, (((1,), (1,)), ((), ())), preferred_element_type=jnp.float32
        )
        scores[:, i * TOK : (i + 1) * TOK] = score
        here = jnp.maximum(score[:, :HS], score[:, HS:])
        best = here if best is None else jnp.maximum(best, here)
    return jnp.broadcast_to(jnp.max(best, axis=1, keepdims=True), (TOK, HS))


def value_pass(values, scores, largest):
    both = jnp.concatenate([largest, largest], axis=1)
    ones = jnp.ones((TOK, HS), jnp.bfloat16)
    total = None
    for i, value in enumerate(values):
        weight = jnp.exp2((scores[:, i * TOK : (i + 1) * TOK] - both) * EXP2_SCALE)
        part = jnp.dot(
            weight.astype(jnp.bfloat16),
            jnp.concatenate([value, ones], axis=1),
            preferred_element_type=jnp.float32,
        )
        total = part if total is None else total + part
    return total[:, :HS], total[:, HS:]


def attend_kernel(own, page_group_ref, facts_ref, q_ref, *refs):
    kv_refs, refs = refs[:10], refs[10:]
    suffix, refs = (refs[:2], refs[2:]) if own else ((), refs)
    if own:
        num_ref, ml_ref, feat, kfeat, scores, top, ml = refs
    else:
        num_ref, feat, kfeat, scores, top, ml = refs
    head = pl.program_id(0)
    wide = (TOK, HS)

    @pl.when(head == 0)
    def _():
        features(own, facts_ref[...].astype(jnp.float32), page_group_ref, feat, kfeat)
        ml[...] = jnp.zeros_like(ml)

    def rows(start):
        pick = slice(start, start + 128)
        later = slice(start + 256, start + 384)
        out = [jnp.concatenate([r[pick, :], r[later, :]], axis=0) for r in kv_refs[:6]]
        for a, b in (kv_refs[6:8], kv_refs[8:10]):
            out.append(jnp.concatenate([a[pick, :], b[pick, :]], axis=0))
        return out

    @pl.when(page_group_ref[0] >= 0)
    def _():
        query = q_ref[...]
        keys = rows(0) + [r[...] for r in suffix[:1]]
        top[...] = score_pass(query, keys, [0] * 8 + [1], feat, kfeat, scores)

    @pl.when(page_group_ref[1] >= 0)
    def _():
        largest = top[...]
        values = rows(128) + [r[...] for r in suffix[1:]]
        num, total = value_pass(values, scores, largest)
        if own:
            num_ref[...] = num
        else:
            cols = pl.ds(pl.multiple_of(head * HS, HS), HS)
            num_ref[0:TOK, cols] = num.astype(jnp.bfloat16)
        lane = lax.broadcasted_iota(jnp.int32, wide, 1)
        ml[...] = jnp.where(lane == head, largest, jnp.where(lane == head + 8, total, ml[...]))

    @pl.when(head == HEADS_DEV - 1)
    def _():
        rows = ml[...].T[0:16, :]
        if own:
            ml_ref[...] = rows
        else:
            high = rows.astype(jnp.bfloat16)
            rest = rows - high.astype(jnp.float32)
            middle = rest.astype(jnp.bfloat16)
            low = (rest - middle.astype(jnp.float32))[0:8, :]
            low = jnp.concatenate([low[:, 0:HS], low[:, HS:]], axis=0).astype(jnp.bfloat16)
            num_ref[TOK : TOK + 16, :] = jnp.concatenate([high, middle, low], axis=1)


def attend(page_group, facts, query, blocks, suffix=()):
    own = bool(suffix)
    count = 9 if own else 8
    width = HEADS_DEV * HS
    tall = lambda array: pl.BlockSpec((array.shape[0], HS), lambda h, *_: (0, h))
    if own:
        out_shape = (
            jax.ShapeDtypeStruct((TOK, width), jnp.float32),
            jax.ShapeDtypeStruct((16, TOK), jnp.float32),
        )
        out_specs = (
            pl.BlockSpec((TOK, HS), lambda h, *_: (0, h)),
            pl.BlockSpec((16, TOK), lambda h, *_: (0, 0)),
        )
    else:
        out_shape = jax.ShapeDtypeStruct((TOK + 16, width), jnp.bfloat16)
        out_specs = pl.BlockSpec((TOK + 16, width), lambda h, *_: (0, 0))
    operands = (query, *blocks, *suffix)
    return pl.pallas_call(
        functools.partial(attend_kernel, own),
        name="attend_own" if own else "attend",
        out_shape=out_shape,
        grid_spec=pltpu.PrefetchScalarGridSpec(
            num_scalar_prefetch=1,
            grid=(HEADS_DEV,),
            in_specs=[pl.BlockSpec((1, 8), lambda h, *_: (0, 0))]
            + [tall(array) for array in operands],
            out_specs=out_specs,
            scratch_shapes=[
                pltpu.VMEM((2, TOK, HS), jnp.bfloat16),
                pltpu.VMEM((9, TOK, HS), jnp.bfloat16),
                pltpu.VMEM((TOK, count * TOK), jnp.float32),
                pltpu.VMEM((TOK, HS), jnp.float32),
                pltpu.VMEM((TOK, HS), jnp.float32),
            ],
        ),
        compiler_params=pltpu.CompilerParams(vmem_limit_bytes=24 << 20),
        cost_estimate=pl.CostEstimate(
            flops=2 * 2 * TOK * TOK * count * HS * HEADS_DEV,
            bytes_accessed=2 * TOK * HS * HEADS_DEV * (2 * count + 3),
            transcendentals=TOK * TOK * count * HEADS_DEV,
        ),
    )(page_group, facts, *operands)


def project_kernel(n0, s0, n1, n2, n3, w_ref, out_ref, att):
    @pl.when(pl.program_id(0) == 0)
    def _():
        tops, sums = [s0[0:8, :]], [s0[8:16, :]]
        for n in (n1, n2, n3):
            piece = n[TOK : TOK + 16, :].astype(jnp.float32)
            low = jnp.concatenate([piece[0:8, 2 * TOK :], piece[8:16, 2 * TOK :]], axis=1)
            tops.append(piece[0:8, :TOK] + piece[0:8, TOK : 2 * TOK] + low)
            sums.append(piece[8:16, :TOK] + piece[8:16, TOK : 2 * TOK])
        best = jnp.maximum(jnp.maximum(tops[0], tops[1]), jnp.maximum(tops[2], tops[3]))
        parts = [jnp.exp2((t - best) * EXP2_SCALE) for t in tops]
        under = sum(p * s for p, s in zip(parts, sums))
        rows = [p / under for p in parts] + [jnp.zeros((96, TOK), jnp.float32)]
        share = jnp.concatenate(rows, axis=0).T
        for h in range(HEADS_DEV):
            cols = slice(h * HS, (h + 1) * HS)
            merged = sum(
                share[:, 8 * i + h : 8 * i + h + 1] * n[0:TOK, cols].astype(jnp.float32)
                for i, n in enumerate((n0, n1, n2, n3))
            )
            att[:, cols] = merged.astype(jnp.bfloat16)

    width = HEADS_DEV * HS
    done = jnp.dot(att[...], w_ref[...], preferred_element_type=jnp.float32)
    out_ref[0] = done[:, :width].astype(jnp.bfloat16)
    out_ref[1] = done[:, width:].astype(jnp.bfloat16)


def project(num, ml, others, weight):
    width = HEADS_DEV * HS
    whole = lambda shape: pl.BlockSpec(shape, lambda j: (0, 0))
    return pl.pallas_call(
        project_kernel,
        name="project",
        out_shape=pltpu.HBM((8, TOK, width), jnp.bfloat16),
        grid=(4,),
        in_specs=[whole((TOK, width)), whole((16, TOK))]
        + [whole((TOK + 16, width))] * 3
        + [pl.BlockSpec((width, 2 * width), lambda j: (0, j))],
        out_specs=pl.BlockSpec((2, TOK, width), lambda j: (j, 0, 0)),
        scratch_shapes=[pltpu.VMEM((TOK, width), jnp.bfloat16)],
        compiler_params=pltpu.CompilerParams(vmem_limit_bytes=24 << 20),
        cost_estimate=pl.CostEstimate(
            flops=2 * TOK * width * D,
            bytes_accessed=2 * (width * D + TOK * D) + 3 * 2 * TOK * width,
            transcendentals=TOK * 20,
        ),
    )(num, ml, *others, weight)


def combine_kernel(parts_ref, residual_ref, gate_ref, combined_ref, sums_ref):
    acc = parts_ref[0].astype(jnp.float32)
    for i in range(1, 8):
        acc = acc + parts_ref[i].astype(jnp.float32)
    combined = residual_ref[...].astype(jnp.float32) + gate_ref[...] * acc
    combined_ref[...] = combined
    first = jnp.sum(combined, axis=1, keepdims=True)
    second = jnp.sum(combined * combined, axis=1, keepdims=True)
    lane = lax.broadcasted_iota(jnp.int32, (HS, HS), 1)
    both = jnp.where(lane == 0, first, jnp.where(lane == 1, second, 0.0))
    rows = both.T[0:8, :]
    for i in range(8):
        sums_ref[i] = rows


def combine(parts, residual, gate):
    width = residual.shape[1]
    return pl.pallas_call(
        combine_kernel,
        name="combine",
        grid=(TOK // HS,),
        in_specs=[
            pl.BlockSpec((8, HS, width), lambda i: (0, i, 0)),
            pl.BlockSpec((HS, width), lambda i: (i, 0)),
            pl.BlockSpec((1, width), lambda i: (0, 0)),
        ],
        out_specs=(
            pl.BlockSpec((HS, width), lambda i: (i, 0)),
            pl.BlockSpec((8, 8, HS), lambda i: (0, 0, i)),
        ),
        out_shape=(
            jax.ShapeDtypeStruct((TOK, width), jnp.float32),
            jax.ShapeDtypeStruct((8, 8, TOK), jnp.float32),
        ),
        compiler_params=pltpu.CompilerParams(vmem_limit_bytes=16 << 20),
    )(parts, residual, gate)


def finish_kernel(combined_ref, sums_ref, shift_ref, scale_ref, stream_ref, mlp_ref):
    total = sums_ref[0]
    for i in range(1, 8):
        total = total + sums_ref[i]
    mean = total[0:1, :] / D
    variance = total[1:2, :] / D - mean * mean
    inverse = 1.0 / jnp.sqrt(variance + 1e-6)
    rows = lax.broadcasted_iota(jnp.int32, (HS, TOK), 0)
    both = jnp.where(rows == 0, mean, jnp.where(rows == 1, inverse, 0.0)).T
    combined = combined_ref[...]
    stream_ref[...] = combined.astype(jnp.bfloat16)
    normed = (combined - both[:, 0:1]) * both[:, 1:2]
    mlp_ref[...] = (normed * (1.0 + scale_ref[...]) + shift_ref[...]).astype(jnp.bfloat16)


def finish(combined, sums, mod_shift, mod_scale):
    shape = jax.ShapeDtypeStruct(combined.shape, jnp.bfloat16)
    return pl.pallas_call(
        finish_kernel,
        name="finish",
        out_shape=(shape, shape),
        compiler_params=pltpu.CompilerParams(vmem_limit_bytes=16 << 20),
    )(combined, sums, mod_shift, mod_scale)


def body(
    queries,
    suffix_keys,
    suffix_values,
    page_cache,
    page_table,
    suffix_lengths,
    request_group,
    residual,
    out_weight,
    attn_gate,
    mod_shift,
    mod_scale,
):
    width = queries.shape[1]
    send = lambda array, dx, dz, dc: lax.ppermute(array, "req", shift(dx, dz, dc))

    ways = (1, 2, -1)
    facts = jnp.concatenate([suffix_lengths, request_group], axis=1)
    their_query = [send(queries, 0, dz, 0) for dz in ways]
    their_facts = [send(facts, 0, dz, 0) for dz in ways]

    pages = page_cache.transpose(0, 2, 1, 3).reshape(2 * TOK, width)
    left, right = send(pages, 1, 0, 0), send(pages, -1, 0, 0)
    over_left = send(left[:TOK], 1, 0, 0)
    over_right = send(right[TOK:], -1, 0, 0)
    near = [pages, left, right]
    blocks = near + [send(array, 0, 0, 1) for array in near] + [over_left, over_right]
    blocks.append(send(over_left, 0, 0, 1))
    blocks.append(send(over_right, 0, 0, 1))

    me = lax.axis_index("req")
    x, z, c = me // (NZ * NC), (me // NC) % NZ, me % NC
    owners = jnp.stack(
        [rank(x - dx, z, c + dc) for dc in (0, 1) for dx in (0, 1, -1)]
        + [rank(x + 2, z, c), rank(x + 2, z, c + 1)]
    )
    slots = (2 * owners[:, None] + jnp.arange(2, dtype=jnp.int32)[None, :]).reshape(16)
    page_group = jnp.sum((page_table[1][None, :] == slots[:, None]).astype(jnp.int32), 1)

    suffix = (suffix_keys, suffix_values)
    others = []
    for i, dz in enumerate(ways):
        num = attend(page_group, their_facts[i], their_query[i], blocks)
        others.append(send(num, 0, -dz, 0))
    num, ml = attend(page_group, facts, queries, blocks, suffix)
    parts = project(num, ml, others, out_weight)
    parts = lax.all_to_all(parts, "tp", 0, 0, tiled=True)
    combined, sums = combine(parts, pltpu.with_memory_space_constraint(residual, pltpu.HBM), attn_gate[None, :])
    sums = lax.all_to_all(sums, "tp", 0, 0, tiled=True)
    return finish(combined, sums, mod_shift[None, :], mod_scale[None, :])


def solution(mesh):
    in_specs = (
        P("req", "tp"),
        P("req", "tp"),
        P("req", "tp"),
        P("req", None, None, "tp"),
        P(),
        P("req", None),
        P("req", None),
        P("req", "tp"),
        P("tp", None),
        P("tp"),
        P("tp"),
        P("tp"),
    )
    out_specs = (P("req", "tp"), P("req", "tp"))

    return jax.shard_map(body, mesh=mesh, in_specs=in_specs, out_specs=out_specs, check_vma=False)
```

```python
import functools
import math

import jax
import jax.numpy as jnp
from jax import lax
from jax.experimental import pallas as pl
from jax.experimental.pallas import tpu as pltpu
from jax.sharding import PartitionSpec as P


D = 5120
HS = 128
SPAN = 64
HEADS_DEV = 5
TOK = 256
BIG = -1e30
INV_SQRT = 1.0 / math.sqrt(HS)
EXP2_SCALE = INV_SQRT * math.log2(math.e)


NX, NZ, NC = 4, 4, 2


def rank(x, z, c):
    return ((x % NX) * NZ + z % NZ) * NC + c % NC


def shift(dx, dz, dc):
    return [
        (rank(x, z, c), rank(x + dx, z + dz, c + dc))
        for x in range(NX)
        for z in range(NZ)
        for c in range(NC)
    ]


def token_facts(facts, shape):
    lane = lax.broadcasted_iota(jnp.int32, facts.shape, 1)
    pick = lambda j: jnp.sum(jnp.where(lane == j, facts, 0.0), axis=1, keepdims=True)
    lens = [pick(j).astype(jnp.int32) for j in range(3)]
    groups = [pick(4 + j).astype(jnp.int32) for j in range(4)]
    pos = lax.broadcasted_iota(jnp.int32, shape, 0)
    e0 = lens[0]
    e1 = e0 + lens[1]
    e2 = e1 + lens[2]
    after0, after1, after2 = pos >= e0, pos >= e1, pos >= e2
    request = jnp.where(after2, 3, jnp.where(after1, 2, jnp.where(after0, 1, 0)))
    start = jnp.where(after2, e2, jnp.where(after1, e1, jnp.where(after0, e0, 0)))
    group = jnp.where(
        after2, groups[3], jnp.where(after1, groups[2], jnp.where(after0, groups[1], groups[0]))
    )
    block = jnp.where(pos - start >= SPAN, 1, 0)
    return request, block, group


def features(own, facts, page_group_ref, feat, kfeat):
    wide = (TOK, HS)
    request, block, group = token_facts(facts, wide)
    lane = lax.broadcasted_iota(jnp.int32, wide, 1)
    row = lax.broadcasted_iota(jnp.int32, wide, 0)
    feat[0] = jnp.where(lane == group, 1.0, 0.0).astype(jnp.bfloat16)
    for i in range(8):
        low, high = page_group_ref[2 * i], page_group_ref[2 * i + 1]
        hidden = (lane < 2) & (lane != jnp.where(row < 128, low, high))
        kfeat[i] = jnp.where(hidden, BIG, 0.0).astype(jnp.bfloat16)
    if own:
        feat[1] = jnp.where(lane == 2 * request + block, 1.0, 0.0).astype(jnp.bfloat16)
        seen = (request == lane // 2) & (block <= lane % 2)
        kfeat[8] = jnp.where((lane < 8) & ~seen, BIG, 0.0).astype(jnp.bfloat16)


def score_pass(query, keys, marks, feat, kfeat, scores):
    best = None
    for i, (key, mark) in enumerate(zip(keys, marks)):
        left = jnp.concatenate([query, feat[mark]], axis=1)
        right = jnp.concatenate([key, kfeat[i]], axis=1)
        score = lax.dot_general(
            left, right, (((1,), (1,)), ((), ())), preferred_element_type=jnp.float32
        )
        scores[:, i * TOK : (i + 1) * TOK] = score
        here = jnp.maximum(score[:, :HS], score[:, HS:])
        best = here if best is None else jnp.maximum(best, here)
    return jnp.broadcast_to(jnp.max(best, axis=1, keepdims=True), (TOK, HS))


def value_pass(values, scores, largest):
    both = jnp.concatenate([largest, largest], axis=1)
    ones = jnp.ones((TOK, HS), jnp.bfloat16)
    total = None
    for i, value in enumerate(values):
        weight = jnp.exp2((scores[:, i * TOK : (i + 1) * TOK] - both) * EXP2_SCALE)
        part = jnp.dot(
            weight.astype(jnp.bfloat16),
            jnp.concatenate([value, ones], axis=1),
            preferred_element_type=jnp.float32,
        )
        total = part if total is None else total + part
    return total[:, :HS], total[:, HS:]


def attend_kernel(own, page_group_ref, facts_ref, q_ref, *refs):
    kv_refs, refs = refs[:16], refs[16:]
    suffix, refs = (refs[:2], refs[2:]) if own else ((), refs)
    if own:
        num_ref, ml_ref, feat, kfeat, scores, top, ml = refs
    else:
        num_ref, feat, kfeat, scores, top, ml = refs
    head = pl.program_id(0)
    wide = (TOK, HS)

    @pl.when(head == 0)
    def _():
        features(own, facts_ref[...].astype(jnp.float32), page_group_ref, feat, kfeat)
        ml[...] = jnp.zeros_like(ml)

    def rows(start):
        pick = slice(start, start + 128)
        return [
            jnp.concatenate([a[pick, :], b[pick, :]], axis=0)
            for a, b in zip(kv_refs[0::2], kv_refs[1::2])
        ]

    @pl.when(page_group_ref[0] >= 0)
    def _():
        query = q_ref[...]
        keys = rows(0) + [r[...] for r in suffix[:1]]
        top[...] = score_pass(query, keys, [0] * 8 + [1], feat, kfeat, scores)

    @pl.when(page_group_ref[1] >= 0)
    def _():
        largest = top[...]
        values = rows(128) + [r[...] for r in suffix[1:]]
        num, total = value_pass(values, scores, largest)
        if own:
            num_ref[...] = num
        else:
            cols = pl.ds(pl.multiple_of(head * HS, HS), HS)
            num_ref[0:TOK, cols] = num.astype(jnp.bfloat16)
        lane = lax.broadcasted_iota(jnp.int32, wide, 1)
        ml[...] = jnp.where(lane == head, largest, jnp.where(lane == head + 8, total, ml[...]))

    @pl.when(head == HEADS_DEV - 1)
    def _():
        rows = ml[...].T[0:16, :]
        if own:
            ml_ref[...] = rows
        else:
            high = rows.astype(jnp.bfloat16)
            rest = rows - high.astype(jnp.float32)
            middle = rest.astype(jnp.bfloat16)
            low = (rest - middle.astype(jnp.float32))[0:8, :]
            low = jnp.concatenate([low[:, 0:HS], low[:, HS:]], axis=0).astype(jnp.bfloat16)
            num_ref[TOK : TOK + 16, :] = jnp.concatenate([high, middle, low], axis=1)


def attend(page_group, facts, query, blocks, suffix=()):
    own = bool(suffix)
    count = 9 if own else 8
    width = HEADS_DEV * HS
    tall = lambda array: pl.BlockSpec((array.shape[0], HS), lambda h, *_: (0, h))
    if own:
        out_shape = (
            jax.ShapeDtypeStruct((TOK, width), jnp.float32),
            jax.ShapeDtypeStruct((16, TOK), jnp.float32),
        )
        out_specs = (
            pl.BlockSpec((TOK, HS), lambda h, *_: (0, h)),
            pl.BlockSpec((16, TOK), lambda h, *_: (0, 0)),
        )
    else:
        out_shape = jax.ShapeDtypeStruct((TOK + 16, width), jnp.bfloat16)
        out_specs = pl.BlockSpec((TOK + 16, width), lambda h, *_: (0, 0))
    operands = (query, *blocks, *suffix)
    return pl.pallas_call(
        functools.partial(attend_kernel, own),
        name="attend_own" if own else "attend",
        out_shape=out_shape,
        grid_spec=pltpu.PrefetchScalarGridSpec(
            num_scalar_prefetch=1,
            grid=(HEADS_DEV,),
            in_specs=[pl.BlockSpec((1, 8), lambda h, *_: (0, 0))]
            + [tall(array) for array in operands],
            out_specs=out_specs,
            scratch_shapes=[
                pltpu.VMEM((2, TOK, HS), jnp.bfloat16),
                pltpu.VMEM((9, TOK, HS), jnp.bfloat16),
                pltpu.VMEM((TOK, count * TOK), jnp.float32),
                pltpu.VMEM((TOK, HS), jnp.float32),
                pltpu.VMEM((TOK, HS), jnp.float32),
            ],
        ),
        compiler_params=pltpu.CompilerParams(vmem_limit_bytes=24 << 20),
        cost_estimate=pl.CostEstimate(
            flops=2 * 2 * TOK * TOK * count * HS * HEADS_DEV,
            bytes_accessed=2 * TOK * HS * HEADS_DEV * (2 * count + 3),
            transcendentals=TOK * TOK * count * HEADS_DEV,
        ),
    )(page_group, facts, *operands)


def project_kernel(n0, s0, n1, n2, n3, w_ref, out_ref, att):
    @pl.when(pl.program_id(0) == 0)
    def _():
        tops, sums = [s0[0:8, :]], [s0[8:16, :]]
        for n in (n1, n2, n3):
            piece = n[TOK : TOK + 16, :].astype(jnp.float32)
            low = jnp.concatenate([piece[0:8, 2 * TOK :], piece[8:16, 2 * TOK :]], axis=1)
            tops.append(piece[0:8, :TOK] + piece[0:8, TOK : 2 * TOK] + low)
            sums.append(piece[8:16, :TOK] + piece[8:16, TOK : 2 * TOK])
        best = jnp.maximum(jnp.maximum(tops[0], tops[1]), jnp.maximum(tops[2], tops[3]))
        parts = [jnp.exp2((t - best) * EXP2_SCALE) for t in tops]
        under = sum(p * s for p, s in zip(parts, sums))
        rows = [p / under for p in parts] + [jnp.zeros((96, TOK), jnp.float32)]
        share = jnp.concatenate(rows, axis=0).T
        for h in range(HEADS_DEV):
            cols = slice(h * HS, (h + 1) * HS)
            merged = sum(
                share[:, 8 * i + h : 8 * i + h + 1] * n[0:TOK, cols].astype(jnp.float32)
                for i, n in enumerate((n0, n1, n2, n3))
            )
            att[:, cols] = merged.astype(jnp.bfloat16)

    width = HEADS_DEV * HS
    done = jnp.dot(att[...], w_ref[...], preferred_element_type=jnp.float32)
    out_ref[0] = done[:, :width].astype(jnp.bfloat16)
    out_ref[1] = done[:, width:].astype(jnp.bfloat16)


def project(num, ml, others, weight):
    width = HEADS_DEV * HS
    whole = lambda shape: pl.BlockSpec(shape, lambda j: (0, 0))
    return pl.pallas_call(
        project_kernel,
        name="project",
        out_shape=pltpu.HBM((8, TOK, width), jnp.bfloat16),
        grid=(4,),
        in_specs=[whole((TOK, width)), whole((16, TOK))]
        + [whole((TOK + 16, width))] * 3
        + [pl.BlockSpec((width, 2 * width), lambda j: (0, j))],
        out_specs=pl.BlockSpec((2, TOK, width), lambda j: (j, 0, 0)),
        scratch_shapes=[pltpu.VMEM((TOK, width), jnp.bfloat16)],
        compiler_params=pltpu.CompilerParams(vmem_limit_bytes=24 << 20),
        cost_estimate=pl.CostEstimate(
            flops=2 * TOK * width * D,
            bytes_accessed=2 * (width * D + TOK * D) + 3 * 2 * TOK * width,
            transcendentals=TOK * 20,
        ),
    )(num, ml, *others, weight)


def combine_kernel(parts_ref, residual_ref, gate_ref, combined_ref, sums_ref):
    acc = parts_ref[0].astype(jnp.float32)
    for i in range(1, 8):
        acc = acc + parts_ref[i].astype(jnp.float32)
    combined = residual_ref[...].astype(jnp.float32) + gate_ref[...] * acc
    combined_ref[...] = combined
    first = jnp.sum(combined, axis=1, keepdims=True)
    second = jnp.sum(combined * combined, axis=1, keepdims=True)
    lane = lax.broadcasted_iota(jnp.int32, (HS, HS), 1)
    both = jnp.where(lane == 0, first, jnp.where(lane == 1, second, 0.0))
    rows = both.T[0:8, :]
    for i in range(8):
        sums_ref[i] = rows


def combine(parts, residual, gate):
    width = residual.shape[1]
    return pl.pallas_call(
        combine_kernel,
        name="combine",
        grid=(TOK // HS,),
        in_specs=[
            pl.BlockSpec((8, HS, width), lambda i: (0, i, 0)),
            pl.BlockSpec((HS, width), lambda i: (i, 0)),
            pl.BlockSpec((1, width), lambda i: (0, 0)),
        ],
        out_specs=(
            pl.BlockSpec((HS, width), lambda i: (i, 0)),
            pl.BlockSpec((8, 8, HS), lambda i: (0, 0, i)),
        ),
        out_shape=(
            jax.ShapeDtypeStruct((TOK, width), jnp.float32),
            jax.ShapeDtypeStruct((8, 8, TOK), jnp.float32),
        ),
        compiler_params=pltpu.CompilerParams(vmem_limit_bytes=16 << 20),
    )(parts, residual, gate)


def finish_kernel(combined_ref, sums_ref, shift_ref, scale_ref, stream_ref, mlp_ref):
    total = sums_ref[0]
    for i in range(1, 8):
        total = total + sums_ref[i]
    mean = total[0:1, :] / D
    variance = total[1:2, :] / D - mean * mean
    inverse = 1.0 / jnp.sqrt(variance + 1e-6)
    rows = lax.broadcasted_iota(jnp.int32, (HS, TOK), 0)
    both = jnp.where(rows == 0, mean, jnp.where(rows == 1, inverse, 0.0)).T
    combined = combined_ref[...]
    stream_ref[...] = combined.astype(jnp.bfloat16)
    normed = (combined - both[:, 0:1]) * both[:, 1:2]
    mlp_ref[...] = (normed * (1.0 + scale_ref[...]) + shift_ref[...]).astype(jnp.bfloat16)


def finish(combined, sums, mod_shift, mod_scale):
    shape = jax.ShapeDtypeStruct(combined.shape, jnp.bfloat16)
    return pl.pallas_call(
        finish_kernel,
        name="finish",
        out_shape=(shape, shape),
        compiler_params=pltpu.CompilerParams(vmem_limit_bytes=16 << 20),
    )(combined, sums, mod_shift, mod_scale)


def body(
    queries,
    suffix_keys,
    suffix_values,
    page_cache,
    page_table,
    suffix_lengths,
    request_group,
    residual,
    out_weight,
    attn_gate,
    mod_shift,
    mod_scale,
):
    width = queries.shape[1]
    send = lambda array, dx, dz, dc: lax.ppermute(array, "req", shift(dx, dz, dc))

    ways = (1, -1, 2)
    facts = jnp.concatenate([suffix_lengths, request_group], axis=1)
    their_query = [send(queries, 0, dz, 0) for dz in ways]
    their_facts = [send(facts, 0, dz, 0) for dz in ways]

    one, two = [
        page.transpose(1, 0, 2).reshape(TOK, width) for page in (page_cache[0], page_cache[1])
    ]
    left_one = send(one, 1, 0, 0)
    right_two = send(two, -1, 0, 0)
    left_two = send(two, 1, 0, 0)
    right_one = send(one, -1, 0, 0)
    over = [send(left_one, 1, 0, 0), send(right_two, -1, 0, 0)]
    near = [one, two, left_one, left_two, right_one, right_two]
    blocks = near + [send(page, 0, 0, 1) for page in near]
    blocks = blocks + over + [send(page, 0, 0, 1) for page in over]

    me = lax.axis_index("req")
    x, z, c = me // (NZ * NC), (me // NC) % NZ, me % NC
    owners = jnp.stack(
        [rank(x - dx, z, c + dc) for dc in (0, 1) for dx in (0, 1, -1)]
        + [rank(x + 2, z, c), rank(x + 2, z, c + 1)]
    )
    slots = (2 * owners[:, None] + jnp.arange(2, dtype=jnp.int32)[None, :]).reshape(16)
    page_group = jnp.sum((page_table[1][None, :] == slots[:, None]).astype(jnp.int32), 1)

    suffix = (suffix_keys, suffix_values)
    others = []
    for i, dz in enumerate(ways):
        num = attend(page_group, their_facts[i], their_query[i], blocks)
        others.append(send(num, 0, -dz, 0))
    num, ml = attend(page_group, facts, queries, blocks, suffix)
    parts = project(num, ml, others, out_weight)
    parts = lax.all_to_all(parts, "tp", 0, 0, tiled=True)
    combined, sums = combine(parts, pltpu.with_memory_space_constraint(residual, pltpu.HBM), attn_gate[None, :])
    sums = lax.all_to_all(sums, "tp", 0, 0, tiled=True)
    return finish(combined, sums, mod_shift[None, :], mod_scale[None, :])


def solution(mesh):
    in_specs = (
        P("req", "tp"),
        P("req", "tp"),
        P("req", "tp"),
        P("req", None, None, "tp"),
        P(),
        P("req", None),
        P("req", None),
        P("req", "tp"),
        P("tp", None),
        P("tp"),
        P("tp"),
        P("tp"),
    )
    out_specs = (P("req", "tp"), P("req", "tp"))

    return jax.shard_map(body, mesh=mesh, in_specs=in_specs, out_specs=out_specs, check_vma=False)
```
